128 devices in a mesh: gz: 16 (over y, z), gy: 8 (over x, core).
Axes of the slice: x: 4, y: 4, z: 4, core: 2. Of those that a mesh axis runs over, the one named last changes fastest.
Arguments:
- patch_force: float32 [16384, 24, 128], P(('gz', 'gy')), may hold values from -36 to 36
- patch_owner: int32 [16384], P(('gz', 'gy')), may hold values from 0 to 127, as said below
- patch_voxel: int32 [16384, 128], P(('gz', 'gy')), may hold values from 0 to 16383
- patch_live: int32 [16384, 8], P(('gz', 'gy')), may hold values from 64 to 128
- voxel_mask: int32 [128, 64, 256], P('gz', 'gy'), may hold values 0 or 1
- element_matrix: float32 [24, 24], replicated, may hold values from -0.2 to 6.5, as said below
Outputs:
- displacement: float32 [24, 128, 64, 256], P(None, 'gz', 'gy')
- residual: float32 [24, 128, 64, 256], P(None, 'gz', 'gy')
The draws below stay inside these ranges and needn't reach their ends.
Inputs may be any that keep to these rules, and one draw needn't show every extreme that they name: `patch_owner`: within the 128 patch blocks of one device no owner appears more than 2 times, and in every device's blocks some owner appears exactly 2 times. `element_matrix`: symmetric positive definite.
All inputs are finite; a program needn't handle non-finite values. No bound on the sum of `voxel_mask` on one device may be relied on, other than what follows from the above.
Results may differ from the reference program's by a relative error of at most 0.00029.
Values sent between devices are 32-bit elements; how exact they have to be, the bound alone decides.
No kernel may reach another device: no remote copies, remote signals or barrier semaphores. Data moves between devices by JAX's collectives and lax.ppermute only.
A program may use at most 128 MiB of HBM per device.

```python
import math
import jax
import jax.numpy as jnp
from jax import lax

CZ = 8
CY = 8
NX = 256
LOADS = 8
PS = 128
PATCH_DEV = 128
ITERS = 2
NZ = 128
NY = 64
PATCHES = 16384
CAP = 2
N_GZ = 16
N_GY = 8
DEVICES = 128


def draw_patch_owner(key, part):
    slot_total = DEVICES * CAP

    def one_block(block_index):
        block_key = jax.random.fold_in(jax.random.fold_in(key, 11), block_index)
        key_base, key_pick, key_order = jax.random.split(block_key, 3)
        slot_index = jnp.arange(slot_total, dtype=jnp.int32)
        owner_of = slot_index // CAP
        level = owner_of // N_GY
        base_score = jax.random.randint(key_base, (slot_total,), 0, 1024, dtype=jnp.int32)
        favored = jax.random.randint(key_pick, (), 0, DEVICES, dtype=jnp.int32)
        score = base_score + 300 * level // max(N_GZ - 1, 1) + jnp.where(owner_of == favored, 1 << 20, 0)
        score = score * slot_total + slot_index
        ignored, picked = lax.top_k(score, PATCH_DEV)
        shuffle = jax.random.permutation(key_order, PATCH_DEV)
        return (picked[shuffle] // CAP).astype(jnp.int32)
    owners = jax.vmap(one_block)(jnp.arange(DEVICES, dtype=jnp.int32))
    return owners.reshape(-1)


def draw_patch_live(key, part):
    key_main, key_row, key_col = jax.random.split(jax.random.fold_in(key, 23), 3)
    counts = jax.random.randint(key_main, (PATCHES, LOADS), PS // 2, PS + 1, dtype=jnp.int32)
    row_pick = jax.random.randint(key_row, (), 0, PATCHES, dtype=jnp.int32)
    col_pick = jax.random.randint(key_col, (), 0, LOADS, dtype=jnp.int32)
    return counts.at[row_pick, col_pick].set(PS)


def draw_patch_force(key, part):
    key_patch, key_chan, key_base = jax.random.split(jax.random.fold_in(key, 37), 3)
    patch_scale = jnp.exp(jax.random.uniform(key_patch, (PATCHES, 1, 1), jnp.float32, math.log(0.3), math.log(3.0)))
    chan_scale = jnp.exp(jax.random.uniform(key_chan, (1, 3 * LOADS, 1), jnp.float32, math.log(0.5), math.log(2.0)))
    base_value = jnp.clip(jax.random.normal(key_base, (PATCHES, 3 * LOADS, PS), jnp.float32), -6.0, 6.0)
    return base_value * patch_scale * chan_scale


def draw_element_matrix(key, part):
    key_off, key_diag = jax.random.split(jax.random.fold_in(key, 41), 2)
    raw_off = jax.random.uniform(key_off, (24, 24), jnp.float32, -0.2, 0.2)
    symmetric = 0.5 * (raw_off + raw_off.T)
    identity = jnp.eye(24, dtype=jnp.float32)
    off_part = symmetric * (1.0 - identity)
    row_weight = jnp.sum(jnp.abs(off_part), axis=1)
    diag_part = 1.25 * row_weight + jax.random.uniform(key_diag, (24,), jnp.float32, 0.2, 0.6)
    return off_part + identity * diag_part[None, :]


def with_ends(result, stream_key, low, top_value):
    longest = result.shape.index(max(result.shape))
    spots = []
    for shift in (0, 1):
        where = [jax.random.randint(jax.random.fold_in(stream_key, axis), (), 0, length) for axis, length in enumerate(result.shape)]
        where[longest] = (where[longest] + shift) % result.shape[longest]
        spots.append(tuple(where))
    return result.at[spots[0]].set(low).at[spots[1]].set(top_value)


def setup_inputs(seed: int = 0) -> dict:
    arg_keys = jax.random.split(jax.random.key(seed), 7)
    patch_force = draw_patch_force(jax.random.fold_in(arg_keys[6], 71), 0)
    patch_owner = draw_patch_owner(jax.random.fold_in(arg_keys[6], 71), 0)
    patch_voxel = with_ends(jax.random.randint(arg_keys[2], (PATCHES, PS), 0, CZ * CY * NX), jax.random.fold_in(arg_keys[2], 1), 0, (CZ * CY * NX) - 1).astype(jnp.int32)
    patch_live = draw_patch_live(jax.random.fold_in(arg_keys[6], 71), 0)
    voxel_mask = with_ends((jax.random.randint(arg_keys[4], (NZ, NY, NX), 0, 2) < 1).astype(jnp.int32), jax.random.fold_in(arg_keys[4], 1), 0, 1)
    element_matrix = draw_element_matrix(jax.random.fold_in(arg_keys[6], 71), 0)
    return dict(patch_force=patch_force, patch_owner=patch_owner, patch_voxel=patch_voxel, patch_live=patch_live, voxel_mask=voxel_mask, element_matrix=element_matrix)


spring = 0.5
highest = lax.Precision.HIGHEST

def plane_terms(padded, modulus, element_matrix, plane_index):
    load_count = padded.shape[0] // 3
    width_rows = padded.shape[2] - 2
    width_cols = padded.shape[3] - 2
    layer = lax.dynamic_slice_in_dim(padded, plane_index, 2, 1)
    corners = []
    for corner_z in (0, 1):
        for corner_y in (0, 1):
            for corner_x in (0, 1):
                corners.append(layer[:, corner_z, corner_y:corner_y + width_rows + 1, corner_x:corner_x + width_cols + 1])
    stacked = jnp.stack(corners, 0).reshape(24, load_count, -1)
    weights = lax.dynamic_index_in_dim(modulus, plane_index, 0, False).reshape(1, 1, -1)
    forces = jnp.einsum('ij,jlq->ilq', element_matrix, stacked, precision=highest) * weights
    forces = forces.reshape(8, 3 * load_count, width_rows + 1, width_cols + 1)
    lower_part = jnp.zeros((3 * load_count, width_rows, width_cols), forces.dtype)
    upper_part = jnp.zeros((3 * load_count, width_rows, width_cols), forces.dtype)
    for corner_y in (0, 1):
        for corner_x in (0, 1):
            start_y = 1 - corner_y
            start_x = 1 - corner_x
            lower_part = lower_part + forces[corner_y * 2 + corner_x][:, start_y:start_y + width_rows, start_x:start_x + width_cols]
            upper_part = upper_part + forces[4 + corner_y * 2 + corner_x][:, start_y:start_y + width_rows, start_x:start_x + width_cols]
    return (lower_part, upper_part)

def assemble(padded, modulus, element_matrix):
    plane_count = modulus.shape[0]
    lower_part, upper_part = lax.map(lambda plane_index: plane_terms(padded, modulus, element_matrix, plane_index), jnp.arange(plane_count, dtype=jnp.int32))
    combined = lower_part[1:] + upper_part[:-1]
    return jnp.transpose(combined, (1, 0, 2, 3))

def gram_local(first, second):
    return jnp.einsum('clq,cmq->lm', first.reshape(3, LOADS, -1), second.reshape(3, LOADS, -1), precision=highest)

def combine(vector_field, matrix):
    mixed = jnp.einsum('clq,lm->cmq', vector_field.reshape(3, LOADS, -1), matrix, precision=highest)
    return mixed.reshape(vector_field.shape)

def solve_small(matrix, target):
    factor = jnp.linalg.cholesky(matrix)
    halfway = lax.linalg.triangular_solve(factor, target, left_side=True, lower=True)
    return lax.linalg.triangular_solve(factor, halfway, left_side=True, lower=True, transpose_a=True)

def reference(patch_force, patch_owner, patch_voxel, patch_live, voxel_mask, element_matrix):
    channels = 3 * LOADS
    owner_z = (patch_owner // N_GY)[:, None]
    owner_y = (patch_owner % N_GY)[:, None]
    coord_z = owner_z * CZ + patch_voxel // (CY * NX)
    coord_y = owner_y * CY + patch_voxel // NX % CY
    coord_x = patch_voxel % NX
    flat_ids = ((coord_z * NY + coord_y) * NX + coord_x).reshape(-1).astype(jnp.int32)
    load_of = jnp.arange(channels, dtype=jnp.int32) % LOADS
    live_count = patch_live[:, load_of]
    keep = jnp.arange(PS, dtype=jnp.int32)[None, None, :] < live_count[:, :, None]
    loaded = jnp.where(keep, patch_force, jnp.zeros_like(patch_force))
    contrib = jnp.transpose(loaded, (1, 0, 2)).reshape(channels, -1)
    nodal_force = jnp.zeros((channels, NZ * NY * NX), patch_force.dtype).at[:, flat_ids].add(contrib)
    nodal_force = nodal_force.reshape(channels, NZ, NY, NX)
    modulus = jnp.pad(voxel_mask.astype(patch_force.dtype), ((1, 0), (1, 0), (1, 0)))
    modulus = modulus.reshape(NZ + 1, (NY + 1) * (NX + 1))

    def apply_operator(vector_field):
        padded = jnp.pad(vector_field, ((0, 0), (1, 1), (1, 1), (1, 1)))
        return assemble(padded, modulus, element_matrix) + spring * vector_field
    displacement = jnp.zeros_like(nodal_force)
    residual = nodal_force
    direction = nodal_force
    norm_gram = gram_local(residual, residual)
    for iteration in range(ITERS):
        applied = apply_operator(direction)
        curvature = gram_local(direction, applied)
        curvature = 0.5 * (curvature + curvature.T)
        step_alpha = solve_small(curvature, norm_gram)
        displacement = displacement + combine(direction, step_alpha)
        residual = residual - combine(applied, step_alpha)
        if iteration + 1 < ITERS:
            norm_next = gram_local(residual, residual)
            step_beta = solve_small(norm_gram, norm_next)
            direction = residual + combine(direction, step_beta)
            norm_gram = norm_next
    return (displacement, residual)
```

```python
import functools
import jax
import jax.numpy as jnp
from jax import lax
from jax.experimental import pallas as pl
from jax.experimental.pallas import tpu as pltpu
from jax.sharding import PartitionSpec as P

LOADS = 8
CH = 24
ROWS = 56
GROUP = 4
AXES = ("gz", "gy")
SPRING = 0.5
F32 = jnp.float32
BF16 = jnp.bfloat16
VMEM_LIMIT = 60 * 1024 * 1024


def vmem():
    return pl.BlockSpec(memory_space=pltpu.VMEM)


def smem():
    return pl.BlockSpec(memory_space=pltpu.SMEM)


def pack_kernel(owner_ref, live_ref, voxel_ref, force_ref, out_ref, count_ref):
    devices = out_ref.shape[0]
    blocks = force_ref.shape[0]
    lane = lax.broadcasted_iota(jnp.int32, (8, 128), 1)

    def clear(i, carry):
        count_ref[i] = 0
        out_ref[i, 48:56, :] = jnp.full((8, 128), -1.0, F32)
        return carry

    lax.fori_loop(0, devices, clear, 0)
    live = live_ref[...]

    def one(p, carry):
        owner = owner_ref[p]
        rank = count_ref[owner]
        count_ref[owner] = rank + 1
        limit = jnp.sum(jnp.where(lane == p, live, 0.0), axis=1, keepdims=True)
        keep = lane.astype(F32) < limit
        for k in range(3):
            base = pl.multiple_of(rank * CH + k * 8, 8)
            out_ref[owner, pl.ds(base, 8), :] = jnp.where(
                keep, force_ref[p, k * 8 : (k + 1) * 8, :], 0.0
            )
        out_ref[owner, pl.ds(48 + rank, 1), :] = voxel_ref[pl.ds(p, 1), :].astype(F32)
        return carry

    lax.fori_loop(0, blocks, one, 0, unroll=4)


def pack(owner, live_t, voxel, force, devices):
    return pl.pallas_call(
        pack_kernel,
        out_shape=jax.ShapeDtypeStruct((devices, ROWS, 128), F32),
        in_specs=[smem(), vmem(), vmem(), vmem()],
        out_specs=vmem(),
        scratch_shapes=[pltpu.SMEM((devices,), jnp.int32)],
        compiler_params=pltpu.CompilerParams(vmem_limit_bytes=VMEM_LIMIT),
        name="pack",
    )(owner, live_t, voxel, force)


def scatter_kernel(valid_ref, recv_ref, *refs):
    outs = refs[:9]
    list_ref, left_ref, right_ref, acc_ref = refs[9:]
    total = valid_ref.shape[0]

    def collect(i, n):
        list_ref[n] = i
        return n + valid_ref[i]

    count = lax.fori_loop(0, total, collect, jnp.int32(0), unroll=8)
    acc_ref[...] = jnp.zeros_like(acc_ref)
    row_x = lax.broadcasted_iota(jnp.int32, (256, 128), 0)
    row_zy = lax.broadcasted_iota(jnp.int32, (64, 128), 0)

    def group(g, carry):
        for j in range(GROUP):
            place = g * GROUP + j
            index = list_ref[jnp.minimum(place, count - 1)]
            source = index // 2
            rank = index % 2
            ids = recv_ref[source, pl.ds(48 + rank, 1), :].astype(jnp.int32)
            zy = jnp.where(place < count, ids // 256, -1)
            x = ids & 255
            hot_x = jnp.where(row_x == x, 1.0, 0.0).astype(BF16)
            right_ref[:, j * 256 : j * 256 + 128] = hot_x
            right_ref[:, j * 256 + 128 : (j + 1) * 256] = hot_x
            hot_zy = jnp.where(row_zy == zy, 1.0, 0.0).astype(BF16)
            value = recv_ref[source, pl.ds(pl.multiple_of(rank * CH, 8), CH), :]
            high = value.astype(BF16).astype(F32)
            low = value - high
            for c in range(CH):
                for half, part in enumerate((high, low)):
                    line = jnp.broadcast_to(part[c : c + 1, :], (16, 128)).astype(BF16)
                    tile = jnp.concatenate([line] * 4, axis=0) * hot_zy
                    at = j * 256 + half * 128
                    left_ref[c * 64 : (c + 1) * 64, at : at + 128] = tile
        for m in range(3):
            part = lax.dot_general(
                left_ref[m * 512 : (m + 1) * 512, :],
                right_ref[...],
                (((1,), (1,)), ((), ())),
                preferred_element_type=F32,
            )
            for h in range(2):
                acc_ref[h, m * 512 : (m + 1) * 512, :] += part[:, h * 128 : (h + 1) * 128]
        return carry

    lax.fori_loop(0, (count + GROUP - 1) // GROUP, group, 0)

    field, z_low, z_high, y_low, y_high, c_ll, c_lh, c_hl, c_hh = outs
    for z in range(8):
        for y in range(8):
            node = jnp.concatenate(
                [
                    jnp.concatenate(
                        [
                            acc_ref[h, pl.ds(k * 512 + z * 8 + y, 8, stride=64), :]
                            for k in range(3)
                        ],
                        axis=0,
                    )
                    for h in range(2)
                ],
                axis=1,
            )
            field[z, y] = node
            if z < 2:
                z_low[z, y] = node
            if z > 5:
                z_high[z - 6, y] = node
            if y < 2:
                y_low[z, y] = node
            if y > 5:
                y_high[z, y - 6] = node
            if z < 2 and y < 2:
                c_ll[z, y] = node
            if z < 2 and y > 5:
                c_lh[z, y - 6] = node
            if z > 5 and y < 2:
                c_hl[z - 6, y] = node
            if z > 5 and y > 5:
                c_hh[z - 6, y - 6] = node


def scatter(valid, recv):
    def shape(a, b):
        return jax.ShapeDtypeStruct((a, b, CH, 256), F32)

    return pl.pallas_call(
        scatter_kernel,
        out_shape=[shape(8, 8), shape(2, 8), shape(2, 8), shape(8, 2), shape(8, 2)]
        + [shape(2, 2)] * 4,
        in_specs=[smem(), vmem()],
        out_specs=[vmem()] * 9,
        scratch_shapes=[
            pltpu.SMEM((valid.shape[0] + 8,), jnp.int32),
            pltpu.VMEM((CH * 64, GROUP * 256), BF16),
            pltpu.VMEM((256, GROUP * 256), BF16),
            pltpu.VMEM((2, CH * 64, 128), F32),
        ],
        compiler_params=pltpu.CompilerParams(vmem_limit_bytes=VMEM_LIMIT),
        name="scatter",
    )(valid, recv)


def shift_down(v, lane):
    return jnp.where(lane == 255, 0.0, pltpu.roll(v, 255, axis=1))


def shift_up(v, lane):
    return jnp.where(lane == 0, 0.0, pltpu.roll(v, 1, axis=1))


def operator_kernel(
    flag_ref, field, z_low, z_high, y_low, y_high, c_ll, c_lh, c_hl, c_hh, mask_ref, k_both, k_high,
    s_out, q_out, gram_out,
    v32, vh, vl, s32, sh, sl, carry_ref, gram_ref,
):
    lane = lax.broadcasted_iota(jnp.int32, (CH, 256), 1)

    def put(full, high, low, z, y, v):
        full[z, y * CH : (y + 1) * CH, :] = v
        both = jnp.concatenate([v, shift_down(v, lane)], axis=0)
        top = both.astype(BF16)
        high[z, y * 48 : (y + 1) * 48, :] = top
        low[z, y * 48 : (y + 1) * 48, :] = (both - top.astype(F32)).astype(BF16)

    def rows(source, z_count, y_count, z_at, y_at):
        def one(z, carry):
            for y in range(y_count):
                put(v32, vh, vl, z + z_at, y + y_at, source[z, y])
            return carry

        lax.fori_loop(0, z_count, one, 0)

    rows(c_ll, 2, 2, 0, 0)
    rows(z_low, 2, 8, 0, 2)
    rows(c_lh, 2, 2, 0, 10)
    rows(y_low, 8, 2, 2, 0)
    rows(field, 8, 8, 2, 2)
    rows(y_high, 8, 2, 2, 10)
    rows(c_hl, 2, 2, 10, 0)
    rows(z_high, 2, 8, 10, 2)
    rows(c_hh, 2, 2, 10, 10)

    def element(high, low, ez, ey):
        def gather(ref):
            return jnp.concatenate(
                [ref[ez, ey * 48 : (ey + 2) * 48, :], ref[ez + 1, ey * 48 : (ey + 2) * 48, :]], axis=0
            )

        first = jnp.dot(k_both[...], gather(high), preferred_element_type=F32)
        second = jnp.dot(k_high[...], gather(low), preferred_element_type=F32)
        force = first[:192] + first[192:] + second
        return force * mask_ref[ez, ey : ey + 1, :]

    def layer(high, low, full, ez, start, stop, finish):
        before = None
        for ey in range(start, stop):
            force = element(high, low, ez, ey)
            if ey > start:
                lower = before[0] + force[0:48] + carry_ref[ey]
                carry_ref[ey] = before[1] + force[96:144]
                value = lower[:CH] + shift_up(lower[CH:], lane)
                finish(ey, value + SPRING * full[ez, ey * CH : (ey + 1) * CH, :])
            before = (force[48:96], force[144:192])

    carry_ref[...] = jnp.zeros_like(carry_ref)

    def first_pass(ez, carry):
        inside = jnp.where(ez == 10, flag_ref[0], 1.0)

        def finish(n, value):
            keep = inside * flag_ref[1] if n == 10 else inside
            put(s32, sh, sl, ez, n, value * keep)

        layer(vh, vl, v32, ez, 0, 11, finish)
        return carry

    lax.fori_loop(0, 11, first_pass, 0)
    carry_ref[...] = jnp.zeros_like(carry_ref)

    def second_pass(ez, carry):
        def finish(n, value):
            q_out[jnp.maximum(ez - 2, 0), n - 2] = value

        layer(sh, sl, s32, ez, 1, 10, finish)
        return carry

    lax.fori_loop(1, 10, second_pass, 0)

    gram_ref[...] = jnp.zeros_like(gram_ref)

    def products(z, carry):
        sums = [None] * 20
        for y in range(8):
            r_row = field[z, y]
            s_row = s32[z + 2, (y + 2) * CH : (y + 3) * CH, :]
            q_row = q_out[z, y]
            s_out[z, y] = s_row
            for k in range(3):
                for h in range(2):
                    r, s, q = (t[k * 8 : (k + 1) * 8, h * 128 : (h + 1) * 128] for t in (r_row, s_row, q_row))
                    for j in range(5):
                        if j == 0:
                            rj, sj, qj = r, s, q
                        else:
                            rj, sj, qj = (pltpu.roll(t, 8 - j, axis=0) for t in (r, s, q))
                        for n, term in enumerate((r * rj, r * sj, s * sj, s * qj)):
                            at = n * 5 + j
                            sums[at] = term if sums[at] is None else sums[at] + term
        for at in range(20):
            gram_ref[at] += sums[at]
        return carry

    lax.fori_loop(0, 8, products, 0)
    spot = lax.broadcasted_iota(jnp.int32, (8, 128), 1)
    packed = jnp.zeros((8, 128), F32)
    for at in range(20):
        packed = packed + jnp.where(spot == at, jnp.sum(gram_ref[at], axis=1, keepdims=True), 0.0)

    def send(i, carry):
        gram_out[i] = packed
        return carry

    lax.fori_loop(0, gram_out.shape[0], send, 0, unroll=8)


def operator(flags, fields, mask, k_both, k_high, devices):
    node = jax.ShapeDtypeStruct((8, 8, CH, 256), F32)
    return pl.pallas_call(
        operator_kernel,
        out_shape=[node, node, jax.ShapeDtypeStruct((devices, 8, 128), F32)],
        in_specs=[smem()] + [vmem()] * 12,
        out_specs=[vmem()] * 3,
        scratch_shapes=[
            pltpu.VMEM((12, 12 * CH, 256), F32),
            pltpu.VMEM((12, 12 * 48, 256), BF16),
            pltpu.VMEM((12, 12 * 48, 256), BF16),
            pltpu.VMEM((11, 11 * CH, 256), F32),
            pltpu.VMEM((11, 11 * 48, 256), BF16),
            pltpu.VMEM((11, 11 * 48, 256), BF16),
            pltpu.VMEM((11, 48, 256), F32),
            pltpu.VMEM((20, 8, 128), F32),
        ],
        compiler_params=pltpu.CompilerParams(vmem_limit_bytes=VMEM_LIMIT),
        name="operator",
    )(flags, *fields, mask, k_both, k_high)


def final_kernel(gram_ref, field, s_ref, q_ref, u_out, r_out, u_half, r_half):
    sub = lax.broadcasted_iota(jnp.int32, (8, 128), 0)
    lane = lax.broadcasted_iota(jnp.int32, (8, 128), 1)
    inside = lane < 8

    total = gram_ref[0]
    for i in range(1, gram_ref.shape[0]):
        total = total + gram_ref[i]

    def column(m, j):
        return jnp.sum(jnp.where(lane == j, m, 0.0), axis=1, keepdims=True)

    def row(m, i):
        return jnp.sum(jnp.where(sub == i, m, 0.0), axis=0, keepdims=True)

    def unpack(base):
        out = jnp.zeros((8, 128), F32)
        for j in range(5):
            out = jnp.where(inside & (((lane - sub) & 7) == j), column(total, base + j), out)
            if 0 < j < 4:
                turned = pltpu.roll(total, j, axis=0)
                out = jnp.where(inside & (((sub - lane) & 7) == j), column(turned, base + j), out)
        return out

    def mul(a, b):
        out = jnp.zeros((8, 128), F32)
        for i in range(8):
            out = out + column(a, i) * row(b, i)
        return out

    def flip(a):
        out = jnp.zeros((8, 128), F32)
        for i in range(8):
            out = jnp.where(lane == i, jnp.sum(jnp.where(lane == sub, row(a, i), 0.0), axis=1, keepdims=True), out)
        return out

    def solve(m, b):
        for i in range(8):
            pivot_row = row(m, i)
            scale = 1.0 / column(pivot_row, i)
            pivot_b = row(b, i) * scale
            pivot_row = pivot_row * scale
            factor = jnp.where(sub == i, 0.0, column(m, i))
            m = jnp.where(sub == i, pivot_row, m - factor * pivot_row)
            b = jnp.where(sub == i, pivot_b, b - factor * pivot_b)
        return b

    rr, w, ss, tt = (unpack(5 * n) for n in range(4))
    alpha = solve(w, rr)
    alpha_t = flip(alpha)
    w_alpha = mul(w, alpha)
    s_alpha = mul(ss, alpha)
    new = rr - w_alpha - flip(w_alpha) + mul(alpha_t, s_alpha)
    beta = solve(rr, new)
    one_beta = beta + jnp.where(lane == sub, 1.0, 0.0)
    turn = flip(one_beta)
    cross = mul(turn, s_alpha)
    w2 = mul(turn, mul(w, one_beta)) - cross - flip(cross) + mul(alpha_t, mul(tt, alpha))
    alpha2 = solve(0.5 * (w2 + flip(w2)), new)
    p_mat = alpha + mul(one_beta, alpha2)
    q_mat = mul(alpha, alpha2)

    def coefficients(mat):
        turned = flip(mat)
        return [
            jnp.broadcast_to(
                jnp.sum(jnp.where(inside & (((lane - sub) & 7) == j), turned, 0.0), axis=1, keepdims=True),
                (8, 128),
            )
            for j in range(8)
        ]

    p_co = coefficients(p_mat)
    q_co = coefficients(q_mat)

    def plane(z, carry):
        for y in range(8):
            for k in range(3):
                for h in range(2):
                    part = (slice(k * 8, (k + 1) * 8), slice(h * 128, (h + 1) * 128))
                    r = field[z, y, part[0], part[1]]
                    s = s_ref[z, y, part[0], part[1]]
                    q = q_ref[z, y, part[0], part[1]]
                    u = None
                    e = r
                    for j in range(8):
                        rj, sj, qj = (t if j == 0 else pltpu.roll(t, 8 - j, axis=0) for t in (r, s, q))
                        term = p_co[j] * rj - q_co[j] * sj
                        u = term if u is None else u + term
                        e = e - p_co[j] * sj + q_co[j] * qj
                    at = pl.ds(k * 512 + z * 8 + y, 8, stride=64)
                    u_half[h, at, :] = u
                    r_half[h, at, :] = e
        return carry

    lax.fori_loop(0, 8, plane, 0)

    def join(i, carry):
        at = pl.ds(pl.multiple_of(i * 64, 64), 64)
        for h in range(2):
            u_out[at, h * 128 : (h + 1) * 128] = u_half[h, at, :]
            r_out[at, h * 128 : (h + 1) * 128] = r_half[h, at, :]
        return carry

    lax.fori_loop(0, CH, join, 0)


def final(gram, field, s, q):
    out = jax.ShapeDtypeStruct((CH * 64, 256), F32)
    return pl.pallas_call(
        final_kernel,
        out_shape=[out, out],
        in_specs=[vmem()] * 4,
        out_specs=[vmem()] * 2,
        scratch_shapes=[pltpu.VMEM((2, CH * 64, 128), F32)] * 2,
        compiler_params=pltpu.CompilerParams(vmem_limit_bytes=VMEM_LIMIT),
        name="final",
    )(gram, field, s, q)


def moved(value, dz, dy):
    nz, ny = lax.axis_size("gz"), lax.axis_size("gy")
    pairs = []
    for z in range(nz):
        for y in range(ny):
            if 0 <= z + dz < nz and 0 <= y + dy < ny:
                pairs.append((z * ny + y, (z + dz) * ny + y + dy))
    return lax.ppermute(value, AXES, pairs)


def body(patch_force, patch_owner, patch_voxel, patch_live, voxel_mask, element_matrix):
    nz, ny = lax.axis_size("gz"), lax.axis_size("gy")
    devices = nz * ny

    send = pack(patch_owner, patch_live.astype(F32).T, patch_voxel, patch_force, devices)
    recv = lax.all_to_all(send, AXES, split_axis=0, concat_axis=0, tiled=True)

    mask = voxel_mask
    mask = jnp.concatenate([moved(mask[6:8], 1, 0), mask, moved(mask[0:1], -1, 0)], axis=0)
    mask = jnp.concatenate([moved(mask[:, 6:8], 0, 1), mask, moved(mask[:, 0:1], 0, -1)], axis=1)
    mask = mask.astype(F32)

    big = jnp.einsum("ij,lm->iljm", element_matrix, jnp.eye(LOADS, dtype=F32)).reshape(192, 192)
    rounded = lax.reduce_precision(big, 8, 7)
    k_high = rounded.astype(BF16)
    k_both = jnp.concatenate([k_high, (big - rounded).astype(BF16)], axis=0)

    valid = (recv[:, 48:50, 0] >= 0).astype(jnp.int32).reshape(-1)
    field, z_low, z_high, y_low, y_high, c_ll, c_lh, c_hl, c_hh = scatter(valid, recv)
    around = (
        field,
        moved(z_high, 1, 0),
        moved(z_low, -1, 0),
        moved(y_high, 0, 1),
        moved(y_low, 0, -1),
        moved(c_hh, 1, 1),
        moved(c_hl, 1, -1),
        moved(c_lh, -1, 1),
        moved(c_ll, -1, -1),
    )
    flags = jnp.stack([lax.axis_index("gz") + 1 < nz, lax.axis_index("gy") + 1 < ny]).astype(F32)
    s, q, gram = operator(flags, around, mask, k_both, k_high, devices)
    gram = lax.all_to_all(gram, AXES, split_axis=0, concat_axis=0, tiled=True)
    u, r = final(gram, field, s, q)
    return u.reshape(CH, 8, 8, 256), r.reshape(CH, 8, 8, 256)


def solution(mesh):
    placed = (
        P(AXES, None, None),
        P(AXES),
        P(AXES, None),
        P(AXES, None),
        P("gz", "gy", None),
        P(),
    )
    return jax.shard_map(
        body,
        mesh=mesh,
        in_specs=placed,
        out_specs=(P(None, "gz", "gy", None), P(None, "gz", "gy", None)),
        check_vma=False,
    )
```

```python
import functools
import jax
import jax.numpy as jnp
from jax import lax
from jax.experimental import pallas as pl
from jax.experimental.pallas import tpu as pltpu
from jax.sharding import PartitionSpec as P

LOADS = 8
CH = 24
GROUP = 4
AXES = ("gz", "gy")
SPRING = 0.5
F32 = jnp.float32
BF16 = jnp.bfloat16
VMEM_LIMIT = 60 * 1024 * 1024


def vmem():
    return pl.BlockSpec(memory_space=pltpu.VMEM)


def smem():
    return pl.BlockSpec(memory_space=pltpu.SMEM)


def pack_kernel(with_ids, owner_ref, live_ref, voxel_ref, force_ref, out_ref, count_ref):
    devices = out_ref.shape[0]
    blocks, width = force_ref.shape[0], force_ref.shape[1]
    lane = lax.broadcasted_iota(jnp.int32, (8, 128), 1)

    def clear(i, carry):
        count_ref[i] = 0
        if with_ids:
            out_ref[i, 2 * width : 2 * width + 8, :] = jnp.full((8, 128), -1.0, F32)
        return carry

    lax.fori_loop(0, devices, clear, 0, unroll=8)
    live = live_ref[...]

    def one(p, carry):
        owner = owner_ref[p]
        rank = count_ref[owner]
        count_ref[owner] = rank + 1
        limit = jnp.sum(jnp.where(lane == p, live, 0.0), axis=1, keepdims=True)
        keep = lane.astype(F32) < limit
        for k in range(0, width, 8):
            base = pl.multiple_of(rank * width + k, 8)
            out_ref[owner, pl.ds(base, 8), :] = jnp.where(keep, force_ref[p, k : k + 8, :], 0.0)
        if with_ids:
            out_ref[owner, pl.ds(2 * width + rank, 1), :] = voxel_ref[pl.ds(p, 1), :].astype(F32)
        return carry

    lax.fori_loop(0, blocks, one, 0, unroll=8)


def pack(owner, live_t, voxel, force, devices, width, place, with_ids):
    blocks = force.shape[0]
    rows = 2 * width + (8 if with_ids else 0)
    return pl.pallas_call(
        functools.partial(pack_kernel, with_ids),
        out_shape=jax.ShapeDtypeStruct((devices, rows, 128), F32),
        grid=(1,),
        in_specs=[
            smem(),
            pl.BlockSpec(live_t.shape, lambda i: (0, 0)),
            pl.BlockSpec(voxel.shape, lambda i: (0, 0)),
            pl.BlockSpec((blocks, width, 128), lambda i: (0, place, 0)),
        ],
        out_specs=pl.BlockSpec((devices, rows, 128), lambda i: (0, 0, 0)),
        scratch_shapes=[pltpu.SMEM((devices,), jnp.int32)],
        compiler_params=pltpu.CompilerParams(vmem_limit_bytes=VMEM_LIMIT),
        name="pack",
    )(owner, live_t, voxel, force)


def add_blocks(count, list_ref, ids_ref, value_of, width, left_ref, right_ref, acc_ref):
    acc_ref[...] = jnp.zeros_like(acc_ref)
    row_x = lax.broadcasted_iota(jnp.int32, (256, 128), 0)
    row_zy = lax.broadcasted_iota(jnp.int32, (64, 128), 0)

    def group(g, carry):
        for j in range(GROUP):
            place = g * GROUP + j
            index = list_ref[jnp.minimum(place, count - 1)]
            source = index & 127
            rank = index >> 7
            ids = ids_ref[rank, pl.ds(source, 1), :]
            zy = jnp.where(place < count, ids >> 8, -1)
            x = ids & 255
            hot_x = jnp.where(row_x == x, 1.0, 0.0).astype(BF16)
            right_ref[:, j * 256 : j * 256 + 128] = hot_x
            right_ref[:, j * 256 + 128 : (j + 1) * 256] = hot_x
            hot_zy = jnp.where(row_zy == zy, 1.0, 0.0).astype(BF16)
            value = value_of(source, rank)
            high = value.astype(BF16).astype(F32)
            low = value - high
            for c in range(width):
                for half, part in enumerate((high, low)):
                    line = jnp.broadcast_to(part[c : c + 1, :], (16, 128)).astype(BF16)
                    tile = jnp.concatenate([line] * 4, axis=0) * hot_zy
                    at = j * 256 + half * 128
                    left_ref[c * 64 : (c + 1) * 64, at : at + 128] = tile
        for m in range(width // 8):
            part = lax.dot_general(
                left_ref[m * 512 : (m + 1) * 512, :],
                right_ref[...],
                (((1,), (1,)), ((), ())),
                preferred_element_type=F32,
            )
            for h in range(2):
                acc_ref[h, m * 512 : (m + 1) * 512, :] += part[:, h * 128 : (h + 1) * 128]
        return carry

    lax.fori_loop(0, (count + GROUP - 1) // GROUP, group, 0)


def node_of(acc_ref, width, z, y):
    return jnp.concatenate(
        [
            jnp.concatenate(
                [acc_ref[h, pl.ds(k * 64 + z * 8 + y, 8, stride=64), :] for k in range(0, width, 8)], axis=0
            )
            for h in range(2)
        ],
        axis=1,
    )


def scatter_first_kernel(
    recv_ref, field, list_out, ids_out, flag_v, flag_s, left_ref, right_ref, acc_ref, sem
):
    width = 8
    rows = 2 * width + 8
    lane = lax.broadcasted_iota(jnp.int32, (8, 128), 1)
    for rank in range(2):
        flags = jnp.zeros((8, 128), jnp.int32)
        for t in range(16):
            ids = recv_ref[pl.ds(t * 8 * rows + 2 * width + rank, 8, stride=rows), :].astype(jnp.int32)
            ids_out[rank, t * 8 : (t + 1) * 8, :] = ids
            flags = jnp.where(lane == t, jnp.where(ids[:, 0:1] >= 0, 1, 0), flags)
        flag_v[rank * 8 : (rank + 1) * 8, :] = flags
    copy = pltpu.make_async_copy(flag_v, flag_s, sem)
    copy.start()
    copy.wait()

    count = jnp.int32(0)
    for rank in range(2):

        def collect(t, n):
            for s in range(8):
                list_out[n] = rank * 128 + t * 8 + s
                n = n + flag_s[rank * 8 + s, t]
            return n

        count = lax.fori_loop(0, 16, collect, count)
    list_out[list_out.shape[0] - 1] = count

    def value_of(source, rank):
        return recv_ref[pl.ds(pl.multiple_of(source * rows + rank * width, 8), width), :]

    add_blocks(count, list_out, ids_out, value_of, width, left_ref, right_ref, acc_ref)
    for z in range(8):
        for y in range(8):
            field[z, y] = node_of(acc_ref, width, z, y)


def scatter_first(recv):
    devices = recv.shape[0]
    return pl.pallas_call(
        scatter_first_kernel,
        out_shape=[
            jax.ShapeDtypeStruct((8, 8, 8, 256), F32),
            jax.ShapeDtypeStruct((2 * devices + 8,), jnp.int32),
            jax.ShapeDtypeStruct((2, devices, 128), jnp.int32),
        ],
        in_specs=[vmem()],
        out_specs=[vmem(), smem(), vmem()],
        scratch_shapes=[
            pltpu.VMEM((16, 128), jnp.int32),
            pltpu.SMEM((16, 128), jnp.int32),
            pltpu.VMEM((512, GROUP * 256), BF16),
            pltpu.VMEM((256, GROUP * 256), BF16),
            pltpu.VMEM((2, 512, 128), F32),
            pltpu.SemaphoreType.DMA,
        ],
        compiler_params=pltpu.CompilerParams(vmem_limit_bytes=VMEM_LIMIT),
        name="scatter_first",
    )(recv.reshape(-1, 128))


def scatter_second_kernel(
    list_ref, ids_ref, recv_ref, part_ref, field, z_low, z_high, y_low, y_high, left_ref, right_ref, acc_ref
):
    width = 16
    count = list_ref[list_ref.shape[0] - 1]

    def value_of(source, rank):
        return recv_ref[source, pl.ds(pl.multiple_of(rank * width, 8), width), :]

    add_blocks(count, list_ref, ids_ref, value_of, width, left_ref, right_ref, acc_ref)
    for z in range(8):
        for y in range(8):
            node = jnp.concatenate([node_of(acc_ref, width, z, y), part_ref[z, y]], axis=0)
            field[z, y] = node
            if z < 2:
                z_low[z, y] = node
            if z > 5:
                z_high[z - 6, y] = node
            if y < 2:
                y_low[z, y] = node
            if y > 5:
                y_high[z, y - 6] = node


def scatter_second(blocks, ids, recv, part):
    def shape(a, b):
        return jax.ShapeDtypeStruct((a, b, CH, 256), F32)

    return pl.pallas_call(
        scatter_second_kernel,
        out_shape=[shape(8, 8), shape(2, 8), shape(2, 8), shape(8, 2), shape(8, 2)],
        in_specs=[smem(), vmem(), vmem(), vmem()],
        out_specs=[vmem()] * 5,
        scratch_shapes=[
            pltpu.VMEM((1024, GROUP * 256), BF16),
            pltpu.VMEM((256, GROUP * 256), BF16),
            pltpu.VMEM((2, 1024, 128), F32),
        ],
        compiler_params=pltpu.CompilerParams(vmem_limit_bytes=VMEM_LIMIT),
        name="scatter_second",
    )(blocks, ids, recv, part)


def shift_down(v, lane):
    return jnp.where(lane == 255, 0.0, pltpu.roll(v, 255, axis=1))


def shift_up(v, lane):
    return jnp.where(lane == 0, 0.0, pltpu.roll(v, 1, axis=1))


def operator_kernel(
    flag_ref, field, z_low, z_high, y_low, y_high, mask_ref, k_both, k_high,
    s_out, q_out, gram_out,
    v32, vh, vl, s32, sh, sl, carry_ref, gram_ref,
):
    lane = lax.broadcasted_iota(jnp.int32, (CH, 256), 1)

    def put(full, high, low, z, y, v):
        full[z, y * CH : (y + 1) * CH, :] = v
        both = jnp.concatenate([v, shift_down(v, lane)], axis=0)
        top = both.astype(BF16)
        high[z, y * 48 : (y + 1) * 48, :] = top
        low[z, y * 48 : (y + 1) * 48, :] = (both - top.astype(F32)).astype(BF16)

    def rows(source, z_count, y_count, z_at, y_at):
        def one(z, carry):
            for y in range(y_count):
                put(v32, vh, vl, z + z_at, y + y_at, source[z, y])
            return carry

        lax.fori_loop(0, z_count, one, 0)

    rows(z_low, 2, 8, 0, 2)
    rows(field, 8, 8, 2, 2)
    rows(z_high, 2, 8, 10, 2)
    rows(y_low, 12, 2, 0, 0)
    rows(y_high, 12, 2, 0, 10)

    def element(high, low, ez, ey):
        def gather(ref):
            return jnp.concatenate(
                [ref[ez, ey * 48 : (ey + 2) * 48, :], ref[ez + 1, ey * 48 : (ey + 2) * 48, :]], axis=0
            )

        first = jnp.dot(k_both[...], gather(high), preferred_element_type=F32)
        second = jnp.dot(k_high[...], gather(low), preferred_element_type=F32)
        force = first[:192] + first[192:] + second
        return force * mask_ref[ez, ey : ey + 1, :]

    def layer(high, low, full, ez, start, stop, finish):
        before = None
        for ey in range(start, stop):
            force = element(high, low, ez, ey)
            if ey > start:
                lower = before[0] + force[0:48] + carry_ref[ey]
                carry_ref[ey] = before[1] + force[96:144]
                value = lower[:CH] + shift_up(lower[CH:], lane)
                finish(ey, value + SPRING * full[ez, ey * CH : (ey + 1) * CH, :])
            before = (force[48:96], force[144:192])

    carry_ref[...] = jnp.zeros_like(carry_ref)

    def first_pass(ez, carry):
        inside = jnp.where(ez == 10, flag_ref[0], 1.0)

        def finish(n, value):
            keep = inside * flag_ref[1] if n == 10 else inside
            put(s32, sh, sl, ez, n, value * keep)

        layer(vh, vl, v32, ez, 0, 11, finish)
        return carry

    lax.fori_loop(0, 11, first_pass, 0)
    carry_ref[...] = jnp.zeros_like(carry_ref)

    def second_pass(ez, carry):
        def finish(n, value):
            q_out[jnp.maximum(ez - 2, 0), n - 2] = value

        layer(sh, sl, s32, ez, 1, 10, finish)
        return carry

    lax.fori_loop(1, 10, second_pass, 0)

    gram_ref[...] = jnp.zeros_like(gram_ref)

    def products(z, carry):
        sums = [None] * 20
        for y in range(8):
            r_row = field[z, y]
            s_row = s32[z + 2, (y + 2) * CH : (y + 3) * CH, :]
            q_row = q_out[z, y]
            s_out[z, y] = s_row
            for k in range(3):
                for h in range(2):
                    r, s, q = (t[k * 8 : (k + 1) * 8, h * 128 : (h + 1) * 128] for t in (r_row, s_row, q_row))
                    for j in range(5):
                        if j == 0:
                            rj, sj, qj = r, s, q
                        else:
                            rj, sj, qj = (pltpu.roll(t, 8 - j, axis=0) for t in (r, s, q))
                        for n, term in enumerate((r * rj, r * sj, s * sj, s * qj)):
                            at = n * 5 + j
                            sums[at] = term if sums[at] is None else sums[at] + term
        for at in range(20):
            gram_ref[at] += sums[at]
        return carry

    lax.fori_loop(0, 8, products, 0)
    spot = lax.broadcasted_iota(jnp.int32, (8, 128), 1) - 16 * lax.broadcasted_iota(jnp.int32, (8, 128), 0)
    packed = [jnp.zeros((8, 128), F32)] * 2
    for at in range(20):
        total = jnp.sum(gram_ref[at], axis=1, keepdims=True)
        packed[at // 16] = packed[at // 16] + jnp.where(spot == at % 16, total, 0.0)
    for h in range(2):
        line = jnp.sum(packed[h], axis=0, keepdims=True)
        gram_out[:, h * 128 : (h + 1) * 128] = jnp.broadcast_to(line, (gram_out.shape[0], 128))


def operator(flags, fields, mask, k_both, k_high, devices):
    node = jax.ShapeDtypeStruct((8, 8, CH, 256), F32)
    return pl.pallas_call(
        operator_kernel,
        out_shape=[node, node, jax.ShapeDtypeStruct((devices, 256), F32)],
        in_specs=[smem()] + [vmem()] * 8,
        out_specs=[vmem()] * 3,
        scratch_shapes=[
            pltpu.VMEM((12, 12 * CH, 256), F32),
            pltpu.VMEM((12, 12 * 48, 256), BF16),
            pltpu.VMEM((12, 12 * 48, 256), BF16),
            pltpu.VMEM((11, 11 * CH, 256), F32),
            pltpu.VMEM((11, 11 * 48, 256), BF16),
            pltpu.VMEM((11, 11 * 48, 256), BF16),
            pltpu.VMEM((11, 48, 256), F32),
            pltpu.VMEM((20, 8, 128), F32),
        ],
        compiler_params=pltpu.CompilerParams(vmem_limit_bytes=VMEM_LIMIT),
        name="operator",
    )(flags, *fields, mask, k_both, k_high)


def final_kernel(
    gram_ref, r_hbm, s_hbm, q_hbm, u_hbm, e_hbm, r_ref, s_ref, q_ref, u_half, e_half, in_sem, out_sem
):
    pairs = ((r_hbm, r_ref), (s_hbm, s_ref), (q_hbm, q_ref))
    loads = [
        [pltpu.make_async_copy(far.at[z], near.at[z], in_sem.at[n, z]) for n, (far, near) in enumerate(pairs)]
        for z in range(8)
    ]
    for z in range(8):
        for n in range(3):
            loads[z][n].start()

    sub = lax.broadcasted_iota(jnp.int32, (8, 128), 0)
    lane = lax.broadcasted_iota(jnp.int32, (8, 128), 1)
    inside = lane < 8
    total = [
        jnp.broadcast_to(jnp.sum(gram_ref[:, h * 128 : (h + 1) * 128], axis=0, keepdims=True), (8, 128))
        for h in range(2)
    ]

    def entry(at, turn):
        here = lane == ((sub - turn) & 7) * 16 + at % 16
        return jnp.sum(jnp.where(here, total[at // 16], 0.0), axis=1, keepdims=True)

    def column(m, j):
        return jnp.sum(jnp.where(lane == j, m, 0.0), axis=1, keepdims=True)

    def row(m, i):
        return jnp.sum(jnp.where(sub == i, m, 0.0), axis=0, keepdims=True)

    def unpack(base):
        out = jnp.zeros((8, 128), F32)
        for j in range(5):
            out = jnp.where(inside & (((lane - sub) & 7) == j), entry(base + j, 0), out)
            if 0 < j < 4:
                out = jnp.where(inside & (((sub - lane) & 7) == j), entry(base + j, j), out)
        return out

    def mul(a, b):
        out = jnp.zeros((8, 128), F32)
        for i in range(8):
            out = out + column(a, i) * row(b, i)
        return out

    def flip(a):
        out = jnp.zeros((8, 128), F32)
        for i in range(8):
            out = jnp.where(lane == i, jnp.sum(jnp.where(lane == sub, row(a, i), 0.0), axis=1, keepdims=True), out)
        return out

    def solve(m, b):
        for i in range(8):
            pivot_row = row(m, i)
            scale = 1.0 / column(pivot_row, i)
            pivot_b = row(b, i) * scale
            pivot_row = pivot_row * scale
            factor = jnp.where(sub == i, 0.0, column(m, i))
            m = jnp.where(sub == i, pivot_row, m - factor * pivot_row)
            b = jnp.where(sub == i, pivot_b, b - factor * pivot_b)
        return b

    rr, w, ss, tt = (unpack(5 * n) for n in range(4))
    alpha = solve(w, rr)
    alpha_t = flip(alpha)
    w_alpha = mul(w, alpha)
    s_alpha = mul(ss, alpha)
    new = rr - w_alpha - flip(w_alpha) + mul(alpha_t, s_alpha)
    beta = solve(rr, new)
    one_beta = beta + jnp.where(lane == sub, 1.0, 0.0)
    turn = flip(one_beta)
    cross = mul(turn, s_alpha)
    w2 = mul(turn, mul(w, one_beta)) - cross - flip(cross) + mul(alpha_t, mul(tt, alpha))
    alpha2 = solve(0.5 * (w2 + flip(w2)), new)
    p_mat = alpha + mul(one_beta, alpha2)
    q_mat = mul(alpha, alpha2)

    wide = lax.broadcasted_iota(jnp.int32, (8, 256), 1)
    segment = wide // 72
    block = (wide - segment * 72) // 8

    def spread(mat):
        turned = flip(mat)
        out = jnp.zeros((8, 256), F32)
        for i in range(8):
            out = jnp.where((wide & 7) == i, column(turned, i), out)
        return out

    p_all, q_all = spread(p_mat), spread(q_mat)
    bands = [
        jnp.where(block == k, p_all, jnp.where(block == 3 + k, -q_all, 0.0)) for k in range(3)
    ] + [jnp.where(block == 3 + k, -p_all, jnp.where(block == 6 + k, q_all, 0.0)) for k in range(3)]
    exact = jnp.concatenate(bands, axis=0)
    segment = lax.broadcasted_iota(jnp.int32, (48, 256), 1) // 72
    high = exact.astype(BF16).astype(F32)
    factor = jnp.where(segment < 2, high, jnp.where(segment == 2, exact - high, 0.0))
    factor = factor[:, :216].astype(BF16)

    stores = []
    for z in range(8):
        for n in range(3):
            loads[z][n].wait()

        for y in range(8):
            r = r_ref[z, y]
            stack = jnp.concatenate([r, s_ref[z, y], q_ref[z, y]], axis=0)
            top = stack.astype(BF16)
            rest = (stack - top.astype(F32)).astype(BF16)
            both = jnp.dot(
                factor, jnp.concatenate([top, rest, top], axis=0), preferred_element_type=F32
            )
            for h in range(2):
                side = slice(h * 128, (h + 1) * 128)
                for k in range(3):
                    at = pl.ds(k * 64 + y, 8, stride=8)
                    u_half[z, h, at, :] = both[k * 8 : (k + 1) * 8, side]
                    e_half[z, h, at, :] = (
                        r[k * 8 : (k + 1) * 8, side] + both[24 + k * 8 : 32 + k * 8, side]
                    )
        for n, (half, far) in enumerate(((u_half, u_hbm), (e_half, e_hbm))):
            for h in range(2):
                copy = pltpu.make_async_copy(
                    half.at[z, h].reshape(CH, 8, 128),
                    far.at[:, z, :, h * 128 : (h + 1) * 128],
                    out_sem.at[n, z, h],
                )
                copy.start()
                stores.append(copy)
    for copy in stores:
        copy.wait()


def final(gram, field, s, q):
    out = jax.ShapeDtypeStruct((CH, 8, 8, 256), F32)
    far = pl.BlockSpec(memory_space=pl.ANY)
    return pl.pallas_call(
        final_kernel,
        out_shape=[out, out],
        in_specs=[vmem()] + [far] * 3,
        out_specs=[far] * 2,
        scratch_shapes=[pltpu.VMEM((8, 8, CH, 256), F32)] * 3
        + [pltpu.VMEM((8, 2, CH * 8, 128), F32)] * 2
        + [pltpu.SemaphoreType.DMA((3, 8)), pltpu.SemaphoreType.DMA((2, 8, 2))],
        compiler_params=pltpu.CompilerParams(vmem_limit_bytes=VMEM_LIMIT),
        name="final",
    )(gram, field, s, q)


def moved(value, axis, step):
    count = lax.axis_size(axis)
    return lax.ppermute(
        value, axis, [(i, i + step) for i in range(count) if 0 <= i + step < count]
    )


def exchange(value):
    return lax.all_to_all(value, AXES, split_axis=0, concat_axis=0, tiled=True)


def body(patch_force, patch_owner, patch_voxel, patch_live, voxel_mask, element_matrix):
    nz, ny = lax.axis_size("gz"), lax.axis_size("gy")
    devices = nz * ny

    live_t = patch_live.astype(F32).T
    packed = functools.partial(pack, patch_owner, live_t, patch_voxel, patch_force, devices)
    first = exchange(packed(8, 2, True))
    second = exchange(packed(16, 0, False))

    mask = voxel_mask
    mask = jnp.concatenate([moved(mask[6:8], "gz", 1), mask, moved(mask[0:1], "gz", -1)], axis=0)
    mask = jnp.concatenate([moved(mask[:, 6:8], "gy", 1), mask, moved(mask[:, 0:1], "gy", -1)], axis=1)
    mask = mask.astype(F32)

    big = jnp.einsum("ij,lm->iljm", element_matrix, jnp.eye(LOADS, dtype=F32)).reshape(192, 192)
    rounded = lax.reduce_precision(big, 8, 7)
    k_high = rounded.astype(BF16)
    k_both = jnp.concatenate([k_high, (big - rounded).astype(BF16)], axis=0)
    flags = jnp.stack([lax.axis_index("gz") + 1 < nz, lax.axis_index("gy") + 1 < ny]).astype(F32)

    part, blocks, ids = scatter_first(first)
    field, z_low, z_high, y_low, y_high = scatter_second(blocks, ids, second, part)
    below, above = moved(z_high, "gz", 1), moved(z_low, "gz", -1)
    y_low = jnp.concatenate([below[:, 0:2], y_low, above[:, 0:2]], axis=0)
    y_high = jnp.concatenate([below[:, 6:8], y_high, above[:, 6:8]], axis=0)
    around = (field, below, above, moved(y_high, "gy", 1), moved(y_low, "gy", -1))
    s, q, gram = operator(flags, around, mask, k_both, k_high, devices)
    return final(exchange(gram), field, s, q)


def solution(mesh):
    placed = (
        P(AXES, None, None),
        P(AXES),
        P(AXES, None),
        P(AXES, None),
        P("gz", "gy", None),
        P(),
    )
    return jax.shard_map(
        body,
        mesh=mesh,
        in_specs=placed,
        out_specs=(P(None, "gz", "gy", None), P(None, "gz", "gy", None)),
        check_vma=False,
    )
```

```python
import functools
import jax
import jax.numpy as jnp
from jax import lax
from jax.experimental import pallas as pl
from jax.experimental.pallas import tpu as pltpu
from jax.sharding import PartitionSpec as P

LOADS = 8
CH = 24
GROUP = 4
UNROLL = 2
AXES = ("gz", "gy")
SPRING = 0.5
F32 = jnp.float32
BF16 = jnp.bfloat16
VMEM_LIMIT = 60 * 1024 * 1024


def vmem():
    return pl.BlockSpec(memory_space=pltpu.VMEM)


def smem():
    return pl.BlockSpec(memory_space=pltpu.SMEM)


def pack_kernel(owner_ref, row_ref, live_ref, voxel_ref, force_hbm, out_ref, force_ref, rank_v, rank_s, sems):
    devices = out_ref.shape[0]
    blocks = force_ref.shape[0]
    lane = lax.broadcasted_iota(jnp.int32, (8, 128), 1)
    load = pltpu.make_async_copy(force_hbm, force_ref, sems.at[0])
    load.start()

    owners = jnp.broadcast_to(row_ref[...], (128, 128)).astype(F32)
    before = lax.broadcasted_iota(jnp.int32, (128, 128), 0) < lax.broadcasted_iota(jnp.int32, (128, 128), 1)
    same = jnp.where((owners.T == owners) & before, 1.0, 0.0)
    rank_v[...] = jnp.broadcast_to(jnp.sum(same, axis=0, keepdims=True), (8, 128)).astype(jnp.int32)
    ranks = pltpu.make_async_copy(rank_v, rank_s, sems.at[1])
    ranks.start()

    def clear(i, carry):
        out_ref[i, 2 * CH : 2 * CH + 8, :] = jnp.full((8, 128), -1.0, F32)
        return carry

    lax.fori_loop(0, devices, clear, 0, unroll=8)
    live = live_ref[...].astype(F32).T
    ranks.wait()
    load.wait()

    def one(p, carry):
        owner = owner_ref[p]
        rank = rank_s[0, p]
        limit = jnp.sum(jnp.where(lane == p, live, 0.0), axis=1, keepdims=True)
        keep = lane.astype(F32) < limit
        for k in range(0, CH, 8):
            base = pl.multiple_of(rank * CH + k, 8)
            out_ref[owner, pl.ds(base, 8), :] = jnp.where(keep, force_ref[p, k : k + 8, :], 0.0)
        out_ref[owner, pl.ds(2 * CH + rank, 1), :] = voxel_ref[pl.ds(p, 1), :].astype(F32)
        return carry

    lax.fori_loop(0, blocks, one, 0, unroll=8)


def pack(owner, live, voxel, force, devices):
    return pl.pallas_call(
        pack_kernel,
        out_shape=jax.ShapeDtypeStruct((devices, 2 * CH + 8, 128), F32),
        in_specs=[smem(), vmem(), vmem(), vmem(), pl.BlockSpec(memory_space=pl.ANY)],
        out_specs=vmem(),
        scratch_shapes=[
            pltpu.VMEM(force.shape, F32),
            pltpu.VMEM((8, 128), jnp.int32),
            pltpu.SMEM((8, 128), jnp.int32),
            pltpu.SemaphoreType.DMA((2,)),
        ],
        compiler_params=pltpu.CompilerParams(vmem_limit_bytes=VMEM_LIMIT),
        name="pack",
    )(owner, owner.reshape(1, -1), live, voxel, force)


def add_blocks(count, list_ref, ids_ref, value_of, acc_ref):
    row_x = lax.broadcasted_iota(jnp.int32, (256, 128), 0)
    row_zy = lax.broadcasted_iota(jnp.int32, (64, 128), 0)
    last = jnp.maximum(count - 1, 0)

    def one(g):
        hots, rights, parts = [], [], []
        for j in range(GROUP):
            place = g * GROUP + j
            index = list_ref[jnp.minimum(place, last)]
            source = index & 127
            rank = index >> 7
            ids = ids_ref[rank, pl.ds(source, 1), :]
            zy = jnp.where(place < count, ids >> 8, -1)
            x = ids & 255
            hot_x = jnp.where(row_x == x, 1.0, 0.0).astype(BF16)
            rights += [hot_x, hot_x]
            hots.append(jnp.where(row_zy == zy, 1.0, 0.0).astype(BF16))
            value = value_of(source, rank)
            high = value.astype(BF16).astype(F32)
            parts.append((high, value - high))
        right = jnp.concatenate(rights, axis=1)
        for m in range(3):
            lines = []
            for c in range(m * 8, (m + 1) * 8):
                tiles = []
                for j in range(GROUP):
                    for part in parts[j]:
                        line = jnp.broadcast_to(part[c : c + 1, :], (16, 128)).astype(BF16)
                        tiles.append(jnp.concatenate([line] * 4, axis=0) * hots[j])
                lines.append(jnp.concatenate(tiles, axis=1))
            product = lax.dot_general(
                jnp.concatenate(lines, axis=0), right, (((1,), (1,)), ((), ())), preferred_element_type=F32
            )
            for h in range(2):
                acc_ref[h, m * 512 : (m + 1) * 512, :] += product[:, h * 128 : (h + 1) * 128]

    def several(i, carry):
        for u in range(UNROLL):
            one(UNROLL * i + u)
        return carry

    lax.fori_loop(0, (count + UNROLL * GROUP - 1) // (UNROLL * GROUP), several, 0)


def scatter_kernel(
    recv_ref, field, z_low, z_high, y_low, y_high,
    list_ref, ids_ref, flag_v, flag_s, acc_ref, sem,
):
    rows = 2 * CH + 8
    lane = lax.broadcasted_iota(jnp.int32, (8, 128), 1)
    for rank in range(2):
        flags = jnp.zeros((8, 128), jnp.int32)
        for t in range(16):
            ids = recv_ref[pl.ds(t * 8 * rows + 2 * CH + rank, 8, stride=rows), :].astype(jnp.int32)
            ids_ref[rank, t * 8 : (t + 1) * 8, :] = ids
            flags = jnp.where(lane == t, jnp.where(ids[:, 0:1] >= 0, 1, 0), flags)
        flag_v[rank * 8 : (rank + 1) * 8, :] = flags
    copy = pltpu.make_async_copy(flag_v, flag_s, sem)
    copy.start()
    acc_ref[...] = jnp.zeros_like(acc_ref)
    copy.wait()

    count = jnp.int32(0)
    for rank in range(2):

        def collect(t, n):
            for s in range(8):
                list_ref[n] = rank * 128 + t * 8 + s
                n = n + flag_s[rank * 8 + s, t]
            return n

        count = lax.fori_loop(0, 16, collect, count)

    def value_of(source, rank):
        return recv_ref[pl.ds(pl.multiple_of(source * rows + rank * CH, 8), CH), :]

    add_blocks(count, list_ref, ids_ref, value_of, acc_ref)
    for z in range(8):
        for y in range(8):
            node = jnp.concatenate(
                [
                    jnp.concatenate(
                        [acc_ref[h, pl.ds(k * 512 + z * 8 + y, 8, stride=64), :] for k in range(3)], axis=0
                    )
                    for h in range(2)
                ],
                axis=1,
            )
            field[z, y] = node
            if z < 2:
                z_low[z, y] = node
            if z > 5:
                z_high[z - 6, y] = node
            if y < 2:
                y_low[z, y] = node
            if y > 5:
                y_high[z, y - 6] = node


def scatter(recv):
    devices = recv.shape[0]

    def shape(a, b):
        return jax.ShapeDtypeStruct((a, b, CH, 256), F32)

    return pl.pallas_call(
        scatter_kernel,
        out_shape=[shape(8, 8), shape(2, 8), shape(2, 8), shape(8, 2), shape(8, 2)],
        in_specs=[vmem()],
        out_specs=[vmem()] * 5,
        scratch_shapes=[
            pltpu.SMEM((2 * devices + 8,), jnp.int32),
            pltpu.VMEM((2, devices, 128), jnp.int32),
            pltpu.VMEM((16, 128), jnp.int32),
            pltpu.SMEM((16, 128), jnp.int32),
            pltpu.VMEM((2, CH * 64, 128), F32),
            pltpu.SemaphoreType.DMA,
        ],
        compiler_params=pltpu.CompilerParams(vmem_limit_bytes=VMEM_LIMIT),
        name="scatter",
    )(recv.reshape(-1, 128))


def shift_down(v, lane):
    return jnp.where(lane == 255, 0.0, pltpu.roll(v, 255, axis=1))


def shift_up(v, lane):
    return jnp.where(lane == 0, 0.0, pltpu.roll(v, 1, axis=1))


def operator_kernel(
    flag_ref, field, z_low, z_high, y_low, y_high, c_low, c_high, mask_ref, k_both, k_high,
    s_out, q_out, gram_out,
    v32, vh, vl, s32, sh, sl, carry_ref, gram_ref,
):
    lane = lax.broadcasted_iota(jnp.int32, (CH, 256), 1)

    def put(full, high, low, z, y, v):
        full[z, y * CH : (y + 1) * CH, :] = v
        both = jnp.concatenate([v, shift_down(v, lane)], axis=0)
        top = both.astype(BF16)
        high[z, y * 48 : (y + 1) * 48, :] = top
        low[z, y * 48 : (y + 1) * 48, :] = (both - top.astype(F32)).astype(BF16)

    def rows(source, z_count, y_count, z_at, y_at):
        def one(z, carry):
            for y in range(y_count):
                put(v32, vh, vl, z + z_at, y + y_at, source[z, y])
            return carry

        lax.fori_loop(0, z_count, one, 0)

    rows(z_low, 2, 8, 0, 2)
    rows(field, 8, 8, 2, 2)
    rows(z_high, 2, 8, 10, 2)
    rows(y_low, 8, 2, 2, 0)
    rows(y_high, 8, 2, 2, 10)
    for part, z_at in ((0, 0), (2, 10)):
        for z in range(2):
            for y in range(2):
                put(v32, vh, vl, z_at + z, y, c_low[part + z, y])
                put(v32, vh, vl, z_at + z, y + 10, c_high[part + z, y])

    def element(high, low, ez, ey):
        def gather(ref):
            return jnp.concatenate(
                [ref[ez, ey * 48 : (ey + 2) * 48, :], ref[ez + 1, ey * 48 : (ey + 2) * 48, :]], axis=0
            )

        first = jnp.dot(k_both[...], gather(high), preferred_element_type=F32)
        second = jnp.dot(k_high[...], gather(low), preferred_element_type=F32)
        force = first[:192] + first[192:] + second
        return force * mask_ref[ez, ey : ey + 1, :]

    def layer(high, low, full, ez, start, stop, finish):
        before = None
        for ey in range(start, stop):
            force = element(high, low, ez, ey)
            if ey > start:
                lower = before[0] + force[0:48] + carry_ref[ey]
                carry_ref[ey] = before[1] + force[96:144]
                value = lower[:CH] + shift_up(lower[CH:], lane)
                finish(ey, value + SPRING * full[ez, ey * CH : (ey + 1) * CH, :])
            before = (force[48:96], force[144:192])

    carry_ref[...] = jnp.zeros_like(carry_ref)

    def first_pass(ez, carry):
        inside = jnp.where(ez == 10, flag_ref[0], 1.0)

        def finish(n, value):
            keep = inside * flag_ref[1] if n == 10 else inside
            put(s32, sh, sl, ez, n, value * keep)

        layer(vh, vl, v32, ez, 0, 11, finish)
        return carry

    lax.fori_loop(0, 11, first_pass, 0)
    carry_ref[...] = jnp.zeros_like(carry_ref)

    def second_pass(ez, carry):
        def finish(n, value):
            q_out[jnp.maximum(ez - 2, 0), n - 2] = value

        layer(sh, sl, s32, ez, 1, 10, finish)
        return carry

    lax.fori_loop(1, 10, second_pass, 0)

    gram_ref[...] = jnp.zeros_like(gram_ref)

    def products(z, carry):
        sums = [None] * 20
        for y in range(8):
            r_row = field[z, y]
            s_row = s32[z + 2, (y + 2) * CH : (y + 3) * CH, :]
            q_row = q_out[z, y]
            s_out[z, y] = s_row
            for k in range(3):
                for h in range(2):
                    r, s, q = (t[k * 8 : (k + 1) * 8, h * 128 : (h + 1) * 128] for t in (r_row, s_row, q_row))
                    for j in range(5):
                        if j == 0:
                            rj, sj, qj = r, s, q
                        else:
                            rj, sj, qj = (pltpu.roll(t, 8 - j, axis=0) for t in (r, s, q))
                        for n, term in enumerate((r * rj, r * sj, s * sj, s * qj)):
                            at = n * 5 + j
                            sums[at] = term if sums[at] is None else sums[at] + term
        for at in range(20):
            gram_ref[at] += sums[at]
        return carry

    lax.fori_loop(0, 8, products, 0)
    spot = lax.broadcasted_iota(jnp.int32, (8, 128), 1) - 16 * lax.broadcasted_iota(jnp.int32, (8, 128), 0)
    packed = [jnp.zeros((8, 128), F32)] * 2
    for at in range(20):
        total = jnp.sum(gram_ref[at], axis=1, keepdims=True)
        packed[at // 16] = packed[at // 16] + jnp.where(spot == at % 16, total, 0.0)
    for h in range(2):
        line = jnp.sum(packed[h], axis=0, keepdims=True)
        gram_out[:, :, h * 128 : (h + 1) * 128] = jnp.broadcast_to(line[None], (gram_out.shape[0], 1, 128))


def operator(flags, fields, mask, k_both, k_high, devices):
    node = jax.ShapeDtypeStruct((8, 8, CH, 256), F32)
    return pl.pallas_call(
        operator_kernel,
        out_shape=[node, node, jax.ShapeDtypeStruct((devices, 1, 256), F32)],
        in_specs=[smem()] + [vmem()] * 10,
        out_specs=[vmem()] * 3,
        scratch_shapes=[
            pltpu.VMEM((12, 12 * CH, 256), F32),
            pltpu.VMEM((12, 12 * 48, 256), BF16),
            pltpu.VMEM((12, 12 * 48, 256), BF16),
            pltpu.VMEM((11, 11 * CH, 256), F32),
            pltpu.VMEM((11, 11 * 48, 256), BF16),
            pltpu.VMEM((11, 11 * 48, 256), BF16),
            pltpu.VMEM((11, 48, 256), F32),
            pltpu.VMEM((20, 8, 128), F32),
        ],
        compiler_params=pltpu.CompilerParams(vmem_limit_bytes=VMEM_LIMIT),
        name="operator",
    )(flags, *fields, mask, k_both, k_high)


def final_kernel(
    gram_ref, r_hbm, s_hbm, q_hbm, u_hbm, e_hbm, r_ref, s_ref, q_ref, u_half, e_half, in_sem, out_sem
):
    pairs = ((r_hbm, r_ref), (s_hbm, s_ref), (q_hbm, q_ref))
    loads = [
        [pltpu.make_async_copy(far.at[z], near.at[z], in_sem.at[n, z]) for n, (far, near) in enumerate(pairs)]
        for z in range(8)
    ]
    for z in range(8):
        for n in range(3):
            loads[z][n].start()

    sub = lax.broadcasted_iota(jnp.int32, (8, 128), 0)
    lane = lax.broadcasted_iota(jnp.int32, (8, 128), 1)
    inside = lane < 8
    total = [
        jnp.broadcast_to(jnp.sum(gram_ref[:, :, h * 128 : (h + 1) * 128], axis=0), (8, 128))
        for h in range(2)
    ]

    def entry(at, turn):
        here = lane == ((sub - turn) & 7) * 16 + at % 16
        return jnp.sum(jnp.where(here, total[at // 16], 0.0), axis=1, keepdims=True)

    def column(m, j):
        return jnp.sum(jnp.where(lane == j, m, 0.0), axis=1, keepdims=True)

    def row(m, i):
        return jnp.sum(jnp.where(sub == i, m, 0.0), axis=0, keepdims=True)

    def unpack(base):
        out = jnp.zeros((8, 128), F32)
        for j in range(5):
            out = jnp.where(inside & (((lane - sub) & 7) == j), entry(base + j, 0), out)
            if 0 < j < 4:
                out = jnp.where(inside & (((sub - lane) & 7) == j), entry(base + j, j), out)
        return out

    def mul(a, b):
        out = jnp.zeros((8, 128), F32)
        for i in range(8):
            out = out + column(a, i) * row(b, i)
        return out

    def flip(a):
        out = jnp.zeros((8, 128), F32)
        for i in range(8):
            out = jnp.where(lane == i, jnp.sum(jnp.where(lane == sub, row(a, i), 0.0), axis=1, keepdims=True), out)
        return out

    def solve(m, b):
        for i in range(8):
            pivot_row = row(m, i)
            scale = 1.0 / column(pivot_row, i)
            pivot_b = row(b, i) * scale
            pivot_row = pivot_row * scale
            factor = jnp.where(sub == i, 0.0, column(m, i))
            m = jnp.where(sub == i, pivot_row, m - factor * pivot_row)
            b = jnp.where(sub == i, pivot_b, b - factor * pivot_b)
        return b

    rr, w, ss, tt = (unpack(5 * n) for n in range(4))
    alpha = solve(w, rr)
    alpha_t = flip(alpha)
    w_alpha = mul(w, alpha)
    s_alpha = mul(ss, alpha)
    new = rr - w_alpha - flip(w_alpha) + mul(alpha_t, s_alpha)
    beta = solve(rr, new)
    one_beta = beta + jnp.where(lane == sub, 1.0, 0.0)
    turn = flip(one_beta)
    cross = mul(turn, s_alpha)
    w2 = mul(turn, mul(w, one_beta)) - cross - flip(cross) + mul(alpha_t, mul(tt, alpha))
    alpha2 = solve(0.5 * (w2 + flip(w2)), new)
    p_mat = alpha + mul(one_beta, alpha2)
    q_mat = mul(alpha, alpha2)

    wide = lax.broadcasted_iota(jnp.int32, (8, 256), 1)
    segment = wide // 72
    block = (wide - segment * 72) // 8

    def spread(mat):
        turned = flip(mat)
        out = jnp.zeros((8, 256), F32)
        for i in range(8):
            out = jnp.where((wide & 7) == i, column(turned, i), out)
        return out

    p_all, q_all = spread(p_mat), spread(q_mat)
    bands = [
        jnp.where(block == k, p_all, jnp.where(block == 3 + k, -q_all, 0.0)) for k in range(3)
    ] + [jnp.where(block == 3 + k, -p_all, jnp.where(block == 6 + k, q_all, 0.0)) for k in range(3)]
    exact = jnp.concatenate(bands, axis=0)
    segment = lax.broadcasted_iota(jnp.int32, (48, 256), 1) // 72
    high = exact.astype(BF16).astype(F32)
    factor = jnp.where(segment < 2, high, jnp.where(segment == 2, exact - high, 0.0))
    factor = factor[:, :216].astype(BF16)

    stores = []
    for z in range(8):
        for n in range(3):
            loads[z][n].wait()

        for y in range(8):
            r = r_ref[z, y]
            stack = jnp.concatenate([r, s_ref[z, y], q_ref[z, y]], axis=0)
            top = stack.astype(BF16)
            rest = (stack - top.astype(F32)).astype(BF16)
            both = jnp.dot(
                factor, jnp.concatenate([top, rest, top], axis=0), preferred_element_type=F32
            )
            for h in range(2):
                side = slice(h * 128, (h + 1) * 128)
                for k in range(3):
                    at = pl.ds(k * 64 + y, 8, stride=8)
                    u_half[z, h, at, :] = both[k * 8 : (k + 1) * 8, side]
                    e_half[z, h, at, :] = (
                        r[k * 8 : (k + 1) * 8, side] + both[24 + k * 8 : 32 + k * 8, side]
                    )
        for n, (half, far) in enumerate(((u_half, u_hbm), (e_half, e_hbm))):
            for h in range(2):
                copy = pltpu.make_async_copy(
                    half.at[z, h].reshape(CH, 8, 128),
                    far.at[:, z, :, h * 128 : (h + 1) * 128],
                    out_sem.at[n, z, h],
                )
                copy.start()
                stores.append(copy)
    for copy in stores:
        copy.wait()


def final(gram, field, s, q):
    out = jax.ShapeDtypeStruct((CH, 8, 8, 256), F32)
    far = pl.BlockSpec(memory_space=pl.ANY)
    return pl.pallas_call(
        final_kernel,
        out_shape=[out, out],
        in_specs=[vmem()] + [far] * 3,
        out_specs=[far] * 2,
        scratch_shapes=[pltpu.VMEM((8, 8, CH, 256), F32)] * 3
        + [pltpu.VMEM((8, 2, CH * 8, 128), F32)] * 2
        + [pltpu.SemaphoreType.DMA((3, 8)), pltpu.SemaphoreType.DMA((2, 8, 2))],
        compiler_params=pltpu.CompilerParams(vmem_limit_bytes=VMEM_LIMIT),
        name="final",
    )(gram, field, s, q)


def moved(value, axis, step):
    count = lax.axis_size(axis)
    return lax.ppermute(
        value, axis, [(i, i + step) for i in range(count) if 0 <= i + step < count]
    )


def exchange(value):
    return lax.all_to_all(value, AXES, split_axis=0, concat_axis=0, tiled=True)


def body(patch_force, patch_owner, patch_voxel, patch_live, voxel_mask, element_matrix):
    nz, ny = lax.axis_size("gz"), lax.axis_size("gy")
    devices = nz * ny

    send = pack(patch_owner, patch_live, patch_voxel, patch_force, devices)
    send, mask = lax.optimization_barrier((send, voxel_mask))
    recv = exchange(send)
    mask = jnp.concatenate([moved(mask[6:8], "gz", 1), mask, moved(mask[0:1], "gz", -1)], axis=0)
    mask = jnp.concatenate([moved(mask[:, 6:8], "gy", 1), mask, moved(mask[:, 0:1], "gy", -1)], axis=1)
    mask = mask.astype(F32)

    big = jnp.einsum("ij,lm->iljm", element_matrix, jnp.eye(LOADS, dtype=F32)).reshape(192, 192)
    rounded = lax.reduce_precision(big, 8, 7)
    k_high = rounded.astype(BF16)
    k_both = jnp.concatenate([k_high, (big - rounded).astype(BF16)], axis=0)
    flags = jnp.stack([lax.axis_index("gz") + 1 < nz, lax.axis_index("gy") + 1 < ny]).astype(F32)

    recv, mask, k_high, k_both, flags = lax.optimization_barrier((recv, mask, k_high, k_both, flags))
    field, z_low, z_high, y_low, y_high = scatter(recv)
    below, above = moved(z_high, "gz", 1), moved(z_low, "gz", -1)
    beside = (moved(y_high, "gy", 1), moved(y_low, "gy", -1))
    low = jnp.concatenate([below[:, 0:2], above[:, 0:2]], axis=0)
    high = jnp.concatenate([below[:, 6:8], above[:, 6:8]], axis=0)
    around = (field, below, above, *beside, moved(high, "gy", 1), moved(low, "gy", -1))
    s, q, gram = operator(flags, around, mask, k_both, k_high, devices)
    return final(exchange(gram), field, s, q)


def solution(mesh):
    placed = (
        P(AXES, None, None),
        P(AXES),
        P(AXES, None),
        P(AXES, None),
        P("gz", "gy", None),
        P(),
    )
    return jax.shard_map(
        body,
        mesh=mesh,
        in_specs=placed,
        out_specs=(P(None, "gz", "gy", None), P(None, "gz", "gy", None)),
        check_vma=False,
    )
```

```python
import functools
import jax
import jax.numpy as jnp
from jax import lax
from jax.experimental import pallas as pl
from jax.experimental.pallas import tpu as pltpu
from jax.sharding import PartitionSpec as P

LOADS = 8
CH = 24
GROUP = 4
UNROLL = 2
AXES = ("gz", "gy")
SPRING = 0.5
F32 = jnp.float32
BF16 = jnp.bfloat16
VMEM_LIMIT = 60 * 1024 * 1024


def vmem():
    return pl.BlockSpec(memory_space=pltpu.VMEM)


def smem():
    return pl.BlockSpec(memory_space=pltpu.SMEM)


def pack_kernel(owner_ref, row_ref, live_ref, voxel_ref, force_hbm, out_ref, force_ref, rank_v, rank_s, sems):
    devices = out_ref.shape[0]
    blocks = force_ref.shape[0]
    lane = lax.broadcasted_iota(jnp.int32, (8, 128), 1)
    load = pltpu.make_async_copy(force_hbm, force_ref, sems.at[0])
    load.start()

    owners = jnp.broadcast_to(row_ref[...], (128, 128)).astype(F32)
    before = lax.broadcasted_iota(jnp.int32, (128, 128), 0) < lax.broadcasted_iota(jnp.int32, (128, 128), 1)
    same = jnp.where((owners.T == owners) & before, 1.0, 0.0)
    rank_v[...] = jnp.broadcast_to(jnp.sum(same, axis=0, keepdims=True), (8, 128)).astype(jnp.int32)
    ranks = pltpu.make_async_copy(rank_v, rank_s, sems.at[1])
    ranks.start()

    def clear(i, carry):
        out_ref[i, 2 * CH : 2 * CH + 8, :] = jnp.full((8, 128), -1.0, F32)
        return carry

    lax.fori_loop(0, devices, clear, 0, unroll=8)
    live = live_ref[...].astype(F32)
    ranks.wait()
    load.wait()

    def one(p, carry):
        owner = owner_ref[p]
        rank = rank_s[0, p]
        limit = jnp.sum(jnp.where(lane == p, live, 0.0), axis=1, keepdims=True)
        keep = lane.astype(F32) < limit
        for k in range(0, CH, 8):
            base = pl.multiple_of(rank * CH + k, 8)
            out_ref[owner, pl.ds(base, 8), :] = jnp.where(keep, force_ref[p, k : k + 8, :], 0.0)
        out_ref[owner, pl.ds(2 * CH + rank, 1), :] = voxel_ref[pl.ds(p, 1), :].astype(F32)
        return carry

    lax.fori_loop(0, blocks, one, 0, unroll=8)


def pack(owner, live, voxel, force, devices):
    return pl.pallas_call(
        pack_kernel,
        out_shape=jax.ShapeDtypeStruct((devices, 2 * CH + 8, 128), F32),
        in_specs=[smem(), vmem(), vmem(), vmem(), pl.BlockSpec(memory_space=pl.ANY)],
        out_specs=vmem(),
        scratch_shapes=[
            pltpu.VMEM(force.shape, F32),
            pltpu.VMEM((8, 128), jnp.int32),
            pltpu.SMEM((8, 128), jnp.int32),
            pltpu.SemaphoreType.DMA((2,)),
        ],
        compiler_params=pltpu.CompilerParams(vmem_limit_bytes=VMEM_LIMIT),
        name="pack",
    )(owner, owner.reshape(1, -1), live.T, voxel, force)


def add_blocks(count, list_ref, ids_ref, value_of, acc_ref):
    row_x = lax.broadcasted_iota(jnp.int32, (256, 128), 0)
    row_zy = lax.broadcasted_iota(jnp.int32, (64, 128), 0)
    last = jnp.maximum(count - 1, 0)

    def one(g):
        hots, rights, parts = [], [], []
        for j in range(GROUP):
            place = g * GROUP + j
            index = list_ref[jnp.minimum(place, last)]
            source = index & 127
            rank = index >> 7
            ids = ids_ref[rank, pl.ds(source, 1), :]
            zy = jnp.where(place < count, ids >> 8, -1)
            x = ids & 255
            hot_x = jnp.where(row_x == x, 1.0, 0.0).astype(BF16)
            rights += [hot_x, hot_x]
            hots.append(jnp.where(row_zy == zy, 1.0, 0.0).astype(BF16))
            value = value_of(source, rank)
            high = value.astype(BF16).astype(F32)
            parts.append((high, value - high))
        right = jnp.concatenate(rights, axis=1)
        for m in range(3):
            lines = []
            for c in range(m * 8, (m + 1) * 8):
                tiles = []
                for j in range(GROUP):
                    for part in parts[j]:
                        line = jnp.broadcast_to(part[c : c + 1, :], (16, 128)).astype(BF16)
                        tiles.append(jnp.concatenate([line] * 4, axis=0) * hots[j])
                lines.append(jnp.concatenate(tiles, axis=1))
            product = lax.dot_general(
                jnp.concatenate(lines, axis=0), right, (((1,), (1,)), ((), ())), preferred_element_type=F32
            )
            for h in range(2):
                acc_ref[h, m * 512 : (m + 1) * 512, :] += product[:, h * 128 : (h + 1) * 128]

    def several(i, carry):
        for u in range(UNROLL):
            one(UNROLL * i + u)
        return carry

    lax.fori_loop(0, (count + UNROLL * GROUP - 1) // (UNROLL * GROUP), several, 0)


def scatter_kernel(
    recv_ref, field, z_low, z_high, y_low, y_high,
    list_ref, ids_ref, flag_v, flag_s, acc_ref, sem,
):
    rows = 2 * CH + 8
    lane = lax.broadcasted_iota(jnp.int32, (8, 128), 1)
    for rank in range(2):
        flags = jnp.zeros((8, 128), jnp.int32)
        for t in range(16):
            ids = recv_ref[pl.ds(t * 8 * rows + 2 * CH + rank, 8, stride=rows), :].astype(jnp.int32)
            ids_ref[rank, t * 8 : (t + 1) * 8, :] = ids
            flags = jnp.where(lane == t, jnp.where(ids[:, 0:1] >= 0, 1, 0), flags)
        flag_v[rank * 8 : (rank + 1) * 8, :] = flags
    copy = pltpu.make_async_copy(flag_v, flag_s, sem)
    copy.start()
    acc_ref[...] = jnp.zeros_like(acc_ref)
    copy.wait()

    count = jnp.int32(0)
    for rank in range(2):

        def collect(t, n):
            for s in range(8):
                list_ref[n] = rank * 128 + t * 8 + s
                n = n + flag_s[rank * 8 + s, t]
            return n

        count = lax.fori_loop(0, 16, collect, count)

    def value_of(source, rank):
        return recv_ref[pl.ds(pl.multiple_of(source * rows + rank * CH, 8), CH), :]

    add_blocks(count, list_ref, ids_ref, value_of, acc_ref)
    for z in range(8):
        for y in range(8):
            node = jnp.concatenate(
                [
                    jnp.concatenate(
                        [acc_ref[h, pl.ds(k * 512 + z * 8 + y, 8, stride=64), :] for k in range(3)], axis=0
                    )
                    for h in range(2)
                ],
                axis=1,
            )
            field[z, y] = node
            if z < 2:
                z_low[z, y] = node
            if z > 5:
                z_high[z - 6, y] = node
            if y < 2:
                y_low[z, y] = node
            if y > 5:
                y_high[z, y - 6] = node


def scatter(recv):
    devices = recv.shape[0]

    def shape(a, b):
        return jax.ShapeDtypeStruct((a, b, CH, 256), F32)

    return pl.pallas_call(
        scatter_kernel,
        out_shape=[shape(8, 8), shape(2, 8), shape(2, 8), shape(8, 2), shape(8, 2)],
        in_specs=[vmem()],
        out_specs=[vmem()] * 5,
        scratch_shapes=[
            pltpu.SMEM((2 * devices + 8,), jnp.int32),
            pltpu.VMEM((2, devices, 128), jnp.int32),
            pltpu.VMEM((16, 128), jnp.int32),
            pltpu.SMEM((16, 128), jnp.int32),
            pltpu.VMEM((2, CH * 64, 128), F32),
            pltpu.SemaphoreType.DMA,
        ],
        compiler_params=pltpu.CompilerParams(vmem_limit_bytes=VMEM_LIMIT),
        name="scatter",
    )(recv.reshape(-1, 128))


def shift_down(v, lane):
    return jnp.where(lane == 255, 0.0, pltpu.roll(v, 255, axis=1))


def shift_up(v, lane):
    return jnp.where(lane == 0, 0.0, pltpu.roll(v, 1, axis=1))


def operator_kernel(
    flag_ref, field, z_low, z_high, y_low, y_high, c_low, c_high, mask_ref, k_both, k_high,
    s_hbm, q_hbm, gram_out,
    v32, vh, vl, s32, sh, sl, q32, carry_ref, gram_ref, sems,
):
    lane = lax.broadcasted_iota(jnp.int32, (CH, 256), 1)

    def put(full, high, low, z, y, v):
        full[z, y * CH : (y + 1) * CH, :] = v
        both = jnp.concatenate([v, shift_down(v, lane)], axis=0)
        top = both.astype(BF16)
        high[z, y * 48 : (y + 1) * 48, :] = top
        low[z, y * 48 : (y + 1) * 48, :] = (both - top.astype(F32)).astype(BF16)

    def rows(source, z_count, y_count, z_at, y_at):
        def one(z, carry):
            for y in range(y_count):
                put(v32, vh, vl, z + z_at, y + y_at, source[z, y])
            return carry

        lax.fori_loop(0, z_count, one, 0)

    rows(z_low, 2, 8, 0, 2)
    rows(field, 8, 8, 2, 2)
    rows(z_high, 2, 8, 10, 2)
    rows(y_low, 8, 2, 2, 0)
    rows(y_high, 8, 2, 2, 10)
    for part, z_at in ((0, 0), (2, 10)):
        for z in range(2):
            for y in range(2):
                put(v32, vh, vl, z_at + z, y, c_low[part + z, y])
                put(v32, vh, vl, z_at + z, y + 10, c_high[part + z, y])

    def element(high, low, ez, ey):
        def gather(ref):
            return jnp.concatenate(
                [ref[ez, ey * 48 : (ey + 2) * 48, :], ref[ez + 1, ey * 48 : (ey + 2) * 48, :]], axis=0
            )

        first = jnp.dot(k_both[...], gather(high), preferred_element_type=F32)
        second = jnp.dot(k_high[...], gather(low), preferred_element_type=F32)
        force = first[:192] + first[192:] + second
        return force * mask_ref[ez, ey : ey + 1, :]

    def layer(high, low, full, ez, start, stop, finish):
        before = None
        for ey in range(start, stop):
            force = element(high, low, ez, ey)
            if ey > start:
                lower = before[0] + force[0:48] + carry_ref[ey]
                carry_ref[ey] = before[1] + force[96:144]
                value = lower[:CH] + shift_up(lower[CH:], lane)
                finish(ey, value + SPRING * full[ez, ey * CH : (ey + 1) * CH, :])
            before = (force[48:96], force[144:192])

    carry_ref[...] = jnp.zeros_like(carry_ref)

    def first_pass(ez, carry):
        inside = jnp.where(ez == 10, flag_ref[0], 1.0)

        def finish(n, value):
            keep = inside * flag_ref[1] if n == 10 else inside
            put(s32, sh, sl, ez, n, value * keep)

        layer(vh, vl, v32, ez, 0, 11, finish)
        return carry

    lax.fori_loop(0, 11, first_pass, 0)
    carry_ref[...] = jnp.zeros_like(carry_ref)
    store_s = pltpu.make_async_copy(s32.at[2:10, 2 * CH : 10 * CH, :], s_hbm, sems.at[0])
    store_s.start()

    def second_pass(ez, carry):
        def finish(n, value):
            q32[jnp.maximum(ez - 2, 0), (n - 2) * CH : (n - 1) * CH, :] = value

        layer(sh, sl, s32, ez, 1, 10, finish)
        return carry

    lax.fori_loop(1, 10, second_pass, 0)
    store_q = pltpu.make_async_copy(q32, q_hbm, sems.at[1])
    store_q.start()

    gram_ref[...] = jnp.zeros_like(gram_ref)

    def products(z, carry):
        sums = [None] * 20
        for y in range(8):
            r_row = field[z, y]
            s_row = s32[z + 2, (y + 2) * CH : (y + 3) * CH, :]
            q_row = q32[z, y * CH : (y + 1) * CH, :]
            for k in range(3):
                for h in range(2):
                    r, s, q = (t[k * 8 : (k + 1) * 8, h * 128 : (h + 1) * 128] for t in (r_row, s_row, q_row))
                    for j in range(5):
                        if j == 0:
                            rj, sj, qj = r, s, q
                        else:
                            rj, sj, qj = (pltpu.roll(t, 8 - j, axis=0) for t in (r, s, q))
                        for n, term in enumerate((r * rj, r * sj, s * sj, s * qj)):
                            at = n * 5 + j
                            sums[at] = term if sums[at] is None else sums[at] + term
        for at in range(20):
            gram_ref[at] += sums[at]
        return carry

    lax.fori_loop(0, 8, products, 0)
    spot = lax.broadcasted_iota(jnp.int32, (8, 128), 1) - 16 * lax.broadcasted_iota(jnp.int32, (8, 128), 0)
    packed = [jnp.zeros((8, 128), F32)] * 2
    for at in range(20):
        total = jnp.sum(gram_ref[at], axis=1, keepdims=True)
        packed[at // 16] = packed[at // 16] + jnp.where(spot == at % 16, total, 0.0)
    for h in range(2):
        line = jnp.sum(packed[h], axis=0, keepdims=True)
        gram_out[:, :, h * 128 : (h + 1) * 128] = jnp.broadcast_to(line[None], (gram_out.shape[0], 1, 128))
    store_s.wait()
    store_q.wait()


def operator(flags, fields, mask, k_both, k_high, devices):
    node = jax.ShapeDtypeStruct((8, 8 * CH, 256), F32)
    far = pl.BlockSpec(memory_space=pl.ANY)
    return pl.pallas_call(
        operator_kernel,
        out_shape=[node, node, jax.ShapeDtypeStruct((devices, 1, 256), F32)],
        in_specs=[smem()] + [vmem()] * 10,
        out_specs=[far, far, vmem()],
        scratch_shapes=[
            pltpu.VMEM((12, 12 * CH, 256), F32),
            pltpu.VMEM((12, 12 * 48, 256), BF16),
            pltpu.VMEM((12, 12 * 48, 256), BF16),
            pltpu.VMEM((11, 11 * CH, 256), F32),
            pltpu.VMEM((11, 11 * 48, 256), BF16),
            pltpu.VMEM((11, 11 * 48, 256), BF16),
            pltpu.VMEM((8, 8 * CH, 256), F32),
            pltpu.VMEM((11, 48, 256), F32),
            pltpu.VMEM((20, 8, 128), F32),
            pltpu.SemaphoreType.DMA((2,)),
        ],
        compiler_params=pltpu.CompilerParams(vmem_limit_bytes=VMEM_LIMIT),
        name="operator",
    )(flags, *fields, mask, k_both, k_high)


def final_kernel(
    gram_ref, r_hbm, s_hbm, q_hbm, u_hbm, e_hbm, r_ref, s_ref, q_ref, u_half, e_half, in_sem, out_sem
):
    pairs = ((r_hbm, r_ref), (s_hbm, s_ref), (q_hbm, q_ref))
    loads = [
        [pltpu.make_async_copy(far.at[z], near.at[z], in_sem.at[n, z]) for n, (far, near) in enumerate(pairs)]
        for z in range(8)
    ]
    for z in range(8):
        for n in range(3):
            loads[z][n].start()

    sub = lax.broadcasted_iota(jnp.int32, (8, 128), 0)
    lane = lax.broadcasted_iota(jnp.int32, (8, 128), 1)
    inside = lane < 8
    total = [
        jnp.broadcast_to(jnp.sum(gram_ref[:, :, h * 128 : (h + 1) * 128], axis=0), (8, 128))
        for h in range(2)
    ]

    def entry(at, turn):
        here = lane == ((sub - turn) & 7) * 16 + at % 16
        return jnp.sum(jnp.where(here, total[at // 16], 0.0), axis=1, keepdims=True)

    def column(m, j):
        return jnp.sum(jnp.where(lane == j, m, 0.0), axis=1, keepdims=True)

    def row(m, i):
        return jnp.sum(jnp.where(sub == i, m, 0.0), axis=0, keepdims=True)

    def unpack(base):
        out = jnp.zeros((8, 128), F32)
        for j in range(5):
            out = jnp.where(inside & (((lane - sub) & 7) == j), entry(base + j, 0), out)
            if 0 < j < 4:
                out = jnp.where(inside & (((sub - lane) & 7) == j), entry(base + j, j), out)
        return out

    def mul(a, b):
        out = jnp.zeros((8, 128), F32)
        for i in range(8):
            out = out + column(a, i) * row(b, i)
        return out

    def flip(a):
        out = jnp.zeros((8, 128), F32)
        for i in range(8):
            out = jnp.where(lane == i, jnp.sum(jnp.where(lane == sub, row(a, i), 0.0), axis=1, keepdims=True), out)
        return out

    def solve(m, b):
        for i in range(8):
            pivot_row = row(m, i)
            scale = 1.0 / column(pivot_row, i)
            pivot_b = row(b, i) * scale
            pivot_row = pivot_row * scale
            factor = jnp.where(sub == i, 0.0, column(m, i))
            m = jnp.where(sub == i, pivot_row, m - factor * pivot_row)
            b = jnp.where(sub == i, pivot_b, b - factor * pivot_b)
        return b

    rr, w, ss, tt = (unpack(5 * n) for n in range(4))
    alpha = solve(w, rr)
    alpha_t = flip(alpha)
    w_alpha = mul(w, alpha)
    s_alpha = mul(ss, alpha)
    new = rr - w_alpha - flip(w_alpha) + mul(alpha_t, s_alpha)
    beta = solve(rr, new)
    one_beta = beta + jnp.where(lane == sub, 1.0, 0.0)
    turn = flip(one_beta)
    cross = mul(turn, s_alpha)
    w2 = mul(turn, mul(w, one_beta)) - cross - flip(cross) + mul(alpha_t, mul(tt, alpha))
    alpha2 = solve(0.5 * (w2 + flip(w2)), new)
    p_mat = alpha + mul(one_beta, alpha2)
    q_mat = mul(alpha, alpha2)

    wide = lax.broadcasted_iota(jnp.int32, (8, 256), 1)
    segment = wide // 72
    block = (wide - segment * 72) // 8

    def spread(mat):
        turned = flip(mat)
        out = jnp.zeros((8, 256), F32)
        for i in range(8):
            out = jnp.where((wide & 7) == i, column(turned, i), out)
        return out

    p_all, q_all = spread(p_mat), spread(q_mat)
    bands = [
        jnp.where(block == k, p_all, jnp.where(block == 3 + k, -q_all, 0.0)) for k in range(3)
    ] + [jnp.where(block == 3 + k, -p_all, jnp.where(block == 6 + k, q_all, 0.0)) for k in range(3)]
    exact = jnp.concatenate(bands, axis=0)
    segment = lax.broadcasted_iota(jnp.int32, (48, 256), 1) // 72
    high = exact.astype(BF16).astype(F32)
    factor = jnp.where(segment < 2, high, jnp.where(segment == 2, exact - high, 0.0))
    factor = factor[:, :216].astype(BF16)

    stores = []
    for z in range(8):
        for n in range(3):
            loads[z][n].wait()

        for y in range(8):
            r = r_ref[z, y]
            at_y = slice(y * CH, (y + 1) * CH)
            stack = jnp.concatenate([r, s_ref[z, at_y, :], q_ref[z, at_y, :]], axis=0)
            top = stack.astype(BF16)
            rest = (stack - top.astype(F32)).astype(BF16)
            both = jnp.dot(
                factor, jnp.concatenate([top, rest, top], axis=0), preferred_element_type=F32
            )
            for h in range(2):
                side = slice(h * 128, (h + 1) * 128)
                for k in range(3):
                    at = pl.ds(k * 64 + y, 8, stride=8)
                    u_half[z, h, at, :] = both[k * 8 : (k + 1) * 8, side]
                    e_half[z, h, at, :] = (
                        r[k * 8 : (k + 1) * 8, side] + both[24 + k * 8 : 32 + k * 8, side]
                    )
        for n, (half, far) in enumerate(((u_half, u_hbm), (e_half, e_hbm))):
            for h in range(2):
                copy = pltpu.make_async_copy(
                    half.at[z, h].reshape(CH, 8, 128),
                    far.at[:, z, :, h * 128 : (h + 1) * 128],
                    out_sem.at[n, z, h],
                )
                copy.start()
                stores.append(copy)
    for copy in stores:
        copy.wait()


def final(gram, field, s, q):
    out = jax.ShapeDtypeStruct((CH, 8, 8, 256), F32)
    far = pl.BlockSpec(memory_space=pl.ANY)
    return pl.pallas_call(
        final_kernel,
        out_shape=[out, out],
        in_specs=[vmem()] + [far] * 3,
        out_specs=[far] * 2,
        scratch_shapes=[pltpu.VMEM((8, 8, CH, 256), F32)]
        + [pltpu.VMEM((8, 8 * CH, 256), F32)] * 2
        + [pltpu.VMEM((8, 2, CH * 8, 128), F32)] * 2
        + [pltpu.SemaphoreType.DMA((3, 8)), pltpu.SemaphoreType.DMA((2, 8, 2))],
        compiler_params=pltpu.CompilerParams(vmem_limit_bytes=VMEM_LIMIT),
        name="final",
    )(gram, field, s, q)


def moved(value, axis, step):
    count = lax.axis_size(axis)
    return lax.ppermute(
        value, axis, [(i, i + step) for i in range(count) if 0 <= i + step < count]
    )


def exchange(value):
    return lax.all_to_all(value, AXES, split_axis=0, concat_axis=0, tiled=True)


def body(patch_force, patch_owner, patch_voxel, patch_live, voxel_mask, element_matrix):
    nz, ny = lax.axis_size("gz"), lax.axis_size("gy")
    devices = nz * ny

    send = pack(patch_owner, patch_live, patch_voxel, patch_force, devices)
    send, mask = lax.optimization_barrier((send, voxel_mask))
    recv = exchange(send)
    mask = jnp.concatenate([moved(mask[6:8], "gz", 1), mask, moved(mask[0:1], "gz", -1)], axis=0)
    mask = jnp.concatenate([moved(mask[:, 6:8], "gy", 1), mask, moved(mask[:, 0:1], "gy", -1)], axis=1)
    mask = mask.astype(F32)

    big = jnp.einsum("ij,lm->iljm", element_matrix, jnp.eye(LOADS, dtype=F32)).reshape(192, 192)
    rounded = lax.reduce_precision(big, 8, 7)
    k_high = rounded.astype(BF16)
    k_both = jnp.concatenate([k_high, (big - rounded).astype(BF16)], axis=0)
    flags = jnp.stack([lax.axis_index("gz") + 1 < nz, lax.axis_index("gy") + 1 < ny]).astype(F32)

    recv, mask, k_high, k_both, flags = lax.optimization_barrier((recv, mask, k_high, k_both, flags))
    field, z_low, z_high, y_low, y_high = scatter(recv)
    below, above = moved(z_high, "gz", 1), moved(z_low, "gz", -1)
    beside = (moved(y_high, "gy", 1), moved(y_low, "gy", -1))
    low = jnp.concatenate([below[:, 0:2], above[:, 0:2]], axis=0)
    high = jnp.concatenate([below[:, 6:8], above[:, 6:8]], axis=0)
    around = (field, below, above, *beside, moved(high, "gy", 1), moved(low, "gy", -1))
    s, q, gram = operator(flags, around, mask, k_both, k_high, devices)
    return final(exchange(gram), field, s, q)


def solution(mesh):
    placed = (
        P(AXES, None, None),
        P(AXES),
        P(AXES, None),
        P(AXES, None),
        P("gz", "gy", None),
        P(),
    )
    return jax.shard_map(
        body,
        mesh=mesh,
        in_specs=placed,
        out_specs=(P(None, "gz", "gy", None), P(None, "gz", "gy", None)),
        check_vma=False,
    )
```

```python
import functools
import jax
import jax.numpy as jnp
from jax import lax
from jax.experimental import pallas as pl
from jax.experimental.pallas import tpu as pltpu
from jax.sharding import PartitionSpec as P

LOADS = 8
CH = 24
GROUP = 4
UNROLL = 2
AXES = ("gz", "gy")
SPRING = 0.5
F32 = jnp.float32
BF16 = jnp.bfloat16
VMEM_LIMIT = 60 * 1024 * 1024


def vmem():
    return pl.BlockSpec(memory_space=pltpu.VMEM)


def smem():
    return pl.BlockSpec(memory_space=pltpu.SMEM)


def pack_kernel(owner_ref, row_ref, live_ref, voxel_ref, force_hbm, out_ref, force_ref, rank_v, rank_s, sems):
    devices = out_ref.shape[0]
    blocks = force_ref.shape[0]
    lane = lax.broadcasted_iota(jnp.int32, (8, 128), 1)
    load = pltpu.make_async_copy(force_hbm, force_ref, sems.at[0])
    load.start()

    owners = jnp.broadcast_to(row_ref[...], (128, 128)).astype(F32)
    before = lax.broadcasted_iota(jnp.int32, (128, 128), 0) < lax.broadcasted_iota(jnp.int32, (128, 128), 1)
    same = jnp.where((owners.T == owners) & before, 1.0, 0.0)
    rank_v[...] = jnp.broadcast_to(jnp.sum(same, axis=0, keepdims=True), (8, 128)).astype(jnp.int32)
    ranks = pltpu.make_async_copy(rank_v, rank_s, sems.at[1])
    ranks.start()

    def clear(i, carry):
        out_ref[i, CH] = jnp.full((2, 128), -1.0, F32)
        return carry

    lax.fori_loop(0, devices, clear, 0, unroll=8)
    live = live_ref[...].astype(F32)
    ranks.wait()
    load.wait()

    def one(p, carry):
        owner = owner_ref[p]
        rank = rank_s[0, p]
        limit = jnp.sum(jnp.where(lane == p, live, 0.0), axis=1, keepdims=True)
        keep = lane.astype(F32) < limit
        for k in range(0, CH, 8):
            part = jnp.where(keep, force_ref[p, k : k + 8, :], 0.0)
            for i in range(4):
                out_ref[owner, rank * (CH // 2) + k // 2 + i] = part[2 * i : 2 * i + 2, :]
        out_ref[owner, CH, pl.ds(rank, 1), :] = voxel_ref[pl.ds(p, 1), :].astype(F32)
        return carry

    lax.fori_loop(0, blocks, one, 0, unroll=8)


def pack(owner, live, voxel, force, devices):
    return pl.pallas_call(
        pack_kernel,
        out_shape=jax.ShapeDtypeStruct((devices, CH + 1, 2, 128), F32),
        in_specs=[smem(), vmem(), vmem(), vmem(), pl.BlockSpec(memory_space=pl.ANY)],
        out_specs=vmem(),
        scratch_shapes=[
            pltpu.VMEM(force.shape, F32),
            pltpu.VMEM((8, 128), jnp.int32),
            pltpu.SMEM((8, 128), jnp.int32),
            pltpu.SemaphoreType.DMA((2,)),
        ],
        compiler_params=pltpu.CompilerParams(vmem_limit_bytes=VMEM_LIMIT),
        name="pack",
    )(owner, owner.reshape(1, -1), live.T, voxel, force)


def add_blocks(count, list_ref, ids_ref, value_of, acc_ref):
    row_x = lax.broadcasted_iota(jnp.int32, (256, 128), 0)
    row_zy = lax.broadcasted_iota(jnp.int32, (64, 128), 0)
    last = jnp.maximum(count - 1, 0)

    def one(g):
        hots, rights, parts = [], [], []
        for j in range(GROUP):
            place = g * GROUP + j
            index = list_ref[jnp.minimum(place, last)]
            source = index & 127
            rank = index >> 7
            ids = ids_ref[rank, pl.ds(source, 1), :]
            zy = jnp.where(place < count, ids >> 8, -1)
            x = ids & 255
            hot_x = jnp.where(row_x == x, 1.0, 0.0).astype(BF16)
            rights += [hot_x, hot_x]
            hots.append(jnp.where(row_zy == zy, 1.0, 0.0).astype(BF16))
            value = value_of(source, rank)
            high = value.astype(BF16).astype(F32)
            parts.append((high, value - high))
        right = jnp.concatenate(rights, axis=1)
        for m in range(3):
            lines = []
            for c in range(m * 8, (m + 1) * 8):
                tiles = []
                for j in range(GROUP):
                    for part in parts[j]:
                        line = jnp.broadcast_to(part[c : c + 1, :], (16, 128)).astype(BF16)
                        tiles.append(jnp.concatenate([line] * 4, axis=0) * hots[j])
                lines.append(jnp.concatenate(tiles, axis=1))
            product = lax.dot_general(
                jnp.concatenate(lines, axis=0), right, (((1,), (1,)), ((), ())), preferred_element_type=F32
            )
            for h in range(2):
                acc_ref[h, m * 512 : (m + 1) * 512, :] += product[:, h * 128 : (h + 1) * 128]

    def several(i, carry):
        for u in range(UNROLL):
            one(UNROLL * i + u)
        return carry

    lax.fori_loop(0, (count + UNROLL * GROUP - 1) // (UNROLL * GROUP), several, 0)


def scatter_kernel(
    recv_ref, field, z_low, z_high, y_low, y_high,
    list_ref, ids_ref, flag_v, flag_s, acc_ref, sem,
):
    lane = lax.broadcasted_iota(jnp.int32, (8, 128), 1)

    def voxels(i, carry):
        pair = recv_ref[i, CH].astype(jnp.int32)
        for rank in range(2):
            ids_ref[rank, pl.ds(i, 1), :] = pair[rank : rank + 1, :]
        return carry

    lax.fori_loop(0, recv_ref.shape[0], voxels, 0, unroll=8)
    for rank in range(2):
        flags = jnp.zeros((8, 128), jnp.int32)
        for t in range(16):
            ids = ids_ref[rank, t * 8 : (t + 1) * 8, :]
            flags = jnp.where(lane == t, jnp.where(ids[:, 0:1] >= 0, 1, 0), flags)
        flag_v[rank * 8 : (rank + 1) * 8, :] = flags
    copy = pltpu.make_async_copy(flag_v, flag_s, sem)
    copy.start()
    acc_ref[...] = jnp.zeros_like(acc_ref)
    copy.wait()

    count = jnp.int32(0)
    for rank in range(2):

        def collect(t, n):
            for s in range(8):
                list_ref[n] = rank * 128 + t * 8 + s
                n = n + flag_s[rank * 8 + s, t]
            return n

        count = lax.fori_loop(0, 16, collect, count)

    def value_of(source, rank):
        half = CH // 2
        return jnp.concatenate([recv_ref[source, rank * half + i] for i in range(half)], axis=0)

    add_blocks(count, list_ref, ids_ref, value_of, acc_ref)
    for z in range(8):
        for y in range(8):
            node = jnp.concatenate(
                [
                    jnp.concatenate(
                        [acc_ref[h, pl.ds(k * 512 + z * 8 + y, 8, stride=64), :] for k in range(3)], axis=0
                    )
                    for h in range(2)
                ],
                axis=1,
            )
            field[z, y] = node
            if z < 2:
                z_low[z, y] = node
            if z > 5:
                z_high[z - 6, y] = node
            if y < 2:
                y_low[z, y] = node
            if y > 5:
                y_high[z, y - 6] = node


def scatter(recv):
    devices = recv.shape[0]

    def shape(a, b):
        return jax.ShapeDtypeStruct((a, b, CH, 256), F32)

    return pl.pallas_call(
        scatter_kernel,
        out_shape=[shape(8, 8), shape(2, 8), shape(2, 8), shape(8, 2), shape(8, 2)],
        in_specs=[vmem()],
        out_specs=[vmem()] * 5,
        scratch_shapes=[
            pltpu.SMEM((2 * devices + 8,), jnp.int32),
            pltpu.VMEM((2, devices, 128), jnp.int32),
            pltpu.VMEM((16, 128), jnp.int32),
            pltpu.SMEM((16, 128), jnp.int32),
            pltpu.VMEM((2, CH * 64, 128), F32),
            pltpu.SemaphoreType.DMA,
        ],
        compiler_params=pltpu.CompilerParams(vmem_limit_bytes=VMEM_LIMIT),
        name="scatter",
    )(recv)


def shift_down(v, lane):
    return jnp.where(lane == 255, 0.0, pltpu.roll(v, 255, axis=1))


def shift_up(v, lane):
    return jnp.where(lane == 0, 0.0, pltpu.roll(v, 1, axis=1))


def operator_kernel(
    flag_ref, field, z_low, z_high, y_low, y_high, c_low, c_high, mask_ref, k_both, k_high,
    s_hbm, q_hbm, gram_out,
    v32, vh, vl, s32, sh, sl, q32, carry_ref, gram_ref, sems,
):
    lane = lax.broadcasted_iota(jnp.int32, (CH, 256), 1)

    def put(full, high, low, z, y, v):
        full[z, y * CH : (y + 1) * CH, :] = v
        both = jnp.concatenate([v, shift_down(v, lane)], axis=0)
        top = both.astype(BF16)
        high[z, y * 48 : (y + 1) * 48, :] = top
        low[z, y * 48 : (y + 1) * 48, :] = (both - top.astype(F32)).astype(BF16)

    def rows(source, z_count, y_count, z_at, y_at):
        def one(z, carry):
            for y in range(y_count):
                put(v32, vh, vl, z + z_at, y + y_at, source[z, y])
            return carry

        lax.fori_loop(0, z_count, one, 0)

    rows(z_low, 2, 8, 0, 2)
    rows(field, 8, 8, 2, 2)
    rows(z_high, 2, 8, 10, 2)
    rows(y_low, 8, 2, 2, 0)
    rows(y_high, 8, 2, 2, 10)
    for part, z_at in ((0, 0), (2, 10)):
        for z in range(2):
            for y in range(2):
                put(v32, vh, vl, z_at + z, y, c_low[part + z, y])
                put(v32, vh, vl, z_at + z, y + 10, c_high[part + z, y])

    def element(high, low, ez, ey):
        def gather(ref):
            return jnp.concatenate(
                [ref[ez, ey * 48 : (ey + 2) * 48, :], ref[ez + 1, ey * 48 : (ey + 2) * 48, :]], axis=0
            )

        first = jnp.dot(k_both[...], gather(high), preferred_element_type=F32)
        second = jnp.dot(k_high[...], gather(low), preferred_element_type=F32)
        force = first[:192] + first[192:] + second
        return force * mask_ref[ez, ey : ey + 1, :]

    def layer(high, low, full, ez, start, stop, finish):
        before = None
        for ey in range(start, stop):
            force = element(high, low, ez, ey)
            if ey > start:
                lower = before[0] + force[0:48] + carry_ref[ey]
                carry_ref[ey] = before[1] + force[96:144]
                value = lower[:CH] + shift_up(lower[CH:], lane)
                finish(ey, value + SPRING * full[ez, ey * CH : (ey + 1) * CH, :])
            before = (force[48:96], force[144:192])

    carry_ref[...] = jnp.zeros_like(carry_ref)

    def first_pass(ez, carry):
        inside = jnp.where(ez == 10, flag_ref[0], 1.0)

        def finish(n, value):
            keep = inside * flag_ref[1] if n == 10 else inside
            put(s32, sh, sl, ez, n, value * keep)

        layer(vh, vl, v32, ez, 0, 11, finish)
        return carry

    lax.fori_loop(0, 11, first_pass, 0)
    carry_ref[...] = jnp.zeros_like(carry_ref)
    store_s = pltpu.make_async_copy(s32.at[2:10, 2 * CH : 10 * CH, :], s_hbm, sems.at[0])
    store_s.start()

    def second_pass(ez, carry):
        def finish(n, value):
            q32[jnp.maximum(ez - 2, 0), (n - 2) * CH : (n - 1) * CH, :] = value

        layer(sh, sl, s32, ez, 1, 10, finish)
        return carry

    lax.fori_loop(1, 10, second_pass, 0)
    store_q = pltpu.make_async_copy(q32, q_hbm, sems.at[1])
    store_q.start()

    gram_ref[...] = jnp.zeros_like(gram_ref)

    def products(z, carry):
        sums = [None] * 20
        for y in range(8):
            r_row = field[z, y]
            s_row = s32[z + 2, (y + 2) * CH : (y + 3) * CH, :]
            q_row = q32[z, y * CH : (y + 1) * CH, :]
            for k in range(3):
                for h in range(2):
                    r, s, q = (t[k * 8 : (k + 1) * 8, h * 128 : (h + 1) * 128] for t in (r_row, s_row, q_row))
                    for j in range(5):
                        if j == 0:
                            rj, sj, qj = r, s, q
                        else:
                            rj, sj, qj = (pltpu.roll(t, 8 - j, axis=0) for t in (r, s, q))
                        for n, term in enumerate((r * rj, r * sj, s * sj, s * qj)):
                            at = n * 5 + j
                            sums[at] = term if sums[at] is None else sums[at] + term
        for at in range(20):
            gram_ref[at] += sums[at]
        return carry

    lax.fori_loop(0, 8, products, 0)
    spot = lax.broadcasted_iota(jnp.int32, (8, 128), 1) - 16 * lax.broadcasted_iota(jnp.int32, (8, 128), 0)
    packed = [jnp.zeros((8, 128), F32)] * 2
    for at in range(20):
        total = jnp.sum(gram_ref[at], axis=1, keepdims=True)
        packed[at // 16] = packed[at // 16] + jnp.where(spot == at % 16, total, 0.0)
    for h in range(2):
        line = jnp.sum(packed[h], axis=0, keepdims=True)
        gram_out[:, :, h * 128 : (h + 1) * 128] = jnp.broadcast_to(line[None], (gram_out.shape[0], 1, 128))
    store_s.wait()
    store_q.wait()


def operator(flags, fields, mask, k_both, k_high, devices):
    node = jax.ShapeDtypeStruct((8, 8 * CH, 256), F32)
    far = pl.BlockSpec(memory_space=pl.ANY)
    return pl.pallas_call(
        operator_kernel,
        out_shape=[node, node, jax.ShapeDtypeStruct((devices, 1, 256), F32)],
        in_specs=[smem()] + [vmem()] * 10,
        out_specs=[far, far, vmem()],
        scratch_shapes=[
            pltpu.VMEM((12, 12 * CH, 256), F32),
            pltpu.VMEM((12, 12 * 48, 256), BF16),
            pltpu.VMEM((12, 12 * 48, 256), BF16),
            pltpu.VMEM((11, 11 * CH, 256), F32),
            pltpu.VMEM((11, 11 * 48, 256), BF16),
            pltpu.VMEM((11, 11 * 48, 256), BF16),
            pltpu.VMEM((8, 8 * CH, 256), F32),
            pltpu.VMEM((11, 48, 256), F32),
            pltpu.VMEM((20, 8, 128), F32),
            pltpu.SemaphoreType.DMA((2,)),
        ],
        compiler_params=pltpu.CompilerParams(vmem_limit_bytes=VMEM_LIMIT),
        name="operator",
    )(flags, *fields, mask, k_both, k_high)


def final_kernel(
    gram_ref, r_hbm, s_hbm, q_hbm, u_hbm, e_hbm, r_ref, s_ref, q_ref, u_half, e_half, in_sem, out_sem
):
    pairs = ((r_hbm, r_ref), (s_hbm, s_ref), (q_hbm, q_ref))
    loads = [
        [pltpu.make_async_copy(far.at[z], near.at[z], in_sem.at[n, z]) for n, (far, near) in enumerate(pairs)]
        for z in range(8)
    ]
    for z in range(8):
        for n in range(3):
            loads[z][n].start()

    sub = lax.broadcasted_iota(jnp.int32, (8, 128), 0)
    lane = lax.broadcasted_iota(jnp.int32, (8, 128), 1)
    inside = lane < 8
    total = [
        jnp.broadcast_to(jnp.sum(gram_ref[:, :, h * 128 : (h + 1) * 128], axis=0), (8, 128))
        for h in range(2)
    ]

    def entry(at, turn):
        here = lane == ((sub - turn) & 7) * 16 + at % 16
        return jnp.sum(jnp.where(here, total[at // 16], 0.0), axis=1, keepdims=True)

    def column(m, j):
        return jnp.sum(jnp.where(lane == j, m, 0.0), axis=1, keepdims=True)

    def row(m, i):
        return jnp.sum(jnp.where(sub == i, m, 0.0), axis=0, keepdims=True)

    def unpack(base):
        out = jnp.zeros((8, 128), F32)
        for j in range(5):
            out = jnp.where(inside & (((lane - sub) & 7) == j), entry(base + j, 0), out)
            if 0 < j < 4:
                out = jnp.where(inside & (((sub - lane) & 7) == j), entry(base + j, j), out)
        return out

    def mul(a, b):
        out = jnp.zeros((8, 128), F32)
        for i in range(8):
            out = out + column(a, i) * row(b, i)
        return out

    def flip(a):
        out = jnp.zeros((8, 128), F32)
        for i in range(8):
            out = jnp.where(lane == i, jnp.sum(jnp.where(lane == sub, row(a, i), 0.0), axis=1, keepdims=True), out)
        return out

    def solve(m, b):
        for i in range(8):
            pivot_row = row(m, i)
            scale = 1.0 / column(pivot_row, i)
            pivot_b = row(b, i) * scale
            pivot_row = pivot_row * scale
            factor = jnp.where(sub == i, 0.0, column(m, i))
            m = jnp.where(sub == i, pivot_row, m - factor * pivot_row)
            b = jnp.where(sub == i, pivot_b, b - factor * pivot_b)
        return b

    rr, w, ss, tt = (unpack(5 * n) for n in range(4))
    alpha = solve(w, rr)
    alpha_t = flip(alpha)
    w_alpha = mul(w, alpha)
    s_alpha = mul(ss, alpha)
    new = rr - w_alpha - flip(w_alpha) + mul(alpha_t, s_alpha)
    beta = solve(rr, new)
    one_beta = beta + jnp.where(lane == sub, 1.0, 0.0)
    turn = flip(one_beta)
    cross = mul(turn, s_alpha)
    w2 = mul(turn, mul(w, one_beta)) - cross - flip(cross) + mul(alpha_t, mul(tt, alpha))
    alpha2 = solve(0.5 * (w2 + flip(w2)), new)
    p_mat = alpha + mul(one_beta, alpha2)
    q_mat = mul(alpha, alpha2)

    wide = lax.broadcasted_iota(jnp.int32, (8, 256), 1)
    segment = wide // 72
    block = (wide - segment * 72) // 8

    def spread(mat):
        turned = flip(mat)
        out = jnp.zeros((8, 256), F32)
        for i in range(8):
            out = jnp.where((wide & 7) == i, column(turned, i), out)
        return out

    p_all, q_all = spread(p_mat), spread(q_mat)
    bands = [
        jnp.where(block == k, p_all, jnp.where(block == 3 + k, -q_all, 0.0)) for k in range(3)
    ] + [jnp.where(block == 3 + k, -p_all, jnp.where(block == 6 + k, q_all, 0.0)) for k in range(3)]
    exact = jnp.concatenate(bands, axis=0)
    segment = lax.broadcasted_iota(jnp.int32, (48, 256), 1) // 72
    high = exact.astype(BF16).astype(F32)
    factor = jnp.where(segment < 2, high, jnp.where(segment == 2, exact - high, 0.0))
    factor = factor[:, :216].astype(BF16)

    stores = []
    for z in range(8):
        for n in range(3):
            loads[z][n].wait()

        for y in range(8):
            r = r_ref[z, y]
            at_y = slice(y * CH, (y + 1) * CH)
            stack = jnp.concatenate([r, s_ref[z, at_y, :], q_ref[z, at_y, :]], axis=0)
            top = stack.astype(BF16)
            rest = (stack - top.astype(F32)).astype(BF16)
            both = jnp.dot(
                factor, jnp.concatenate([top, rest, top], axis=0), preferred_element_type=F32
            )
            for h in range(2):
                side = slice(h * 128, (h + 1) * 128)
                for k in range(3):
                    at = pl.ds(k * 64 + y, 8, stride=8)
                    u_half[z, h, at, :] = both[k * 8 : (k + 1) * 8, side]
                    e_half[z, h, at, :] = (
                        r[k * 8 : (k + 1) * 8, side] + both[24 + k * 8 : 32 + k * 8, side]
                    )
        for n, (half, far) in enumerate(((u_half, u_hbm), (e_half, e_hbm))):
            for h in range(2):
                copy = pltpu.make_async_copy(
                    half.at[z, h].reshape(CH, 8, 128),
                    far.at[:, z, :, h * 128 : (h + 1) * 128],
                    out_sem.at[n, z, h],
                )
                copy.start()
                stores.append(copy)
    for copy in stores:
        copy.wait()


def final(gram, field, s, q):
    out = jax.ShapeDtypeStruct((CH, 8, 8, 256), F32)
    far = pl.BlockSpec(memory_space=pl.ANY)
    return pl.pallas_call(
        final_kernel,
        out_shape=[out, out],
        in_specs=[vmem()] + [far] * 3,
        out_specs=[far] * 2,
        scratch_shapes=[pltpu.VMEM((8, 8, CH, 256), F32)]
        + [pltpu.VMEM((8, 8 * CH, 256), F32)] * 2
        + [pltpu.VMEM((8, 2, CH * 8, 128), F32)] * 2
        + [pltpu.SemaphoreType.DMA((3, 8)), pltpu.SemaphoreType.DMA((2, 8, 2))],
        compiler_params=pltpu.CompilerParams(vmem_limit_bytes=VMEM_LIMIT),
        name="final",
    )(gram, field, s, q)


def moved(value, axis, step):
    count = lax.axis_size(axis)
    return lax.ppermute(
        value, axis, [(i, i + step) for i in range(count) if 0 <= i + step < count]
    )


def exchange(value):
    return lax.all_to_all(value, AXES, split_axis=0, concat_axis=0, tiled=True)


def body(patch_force, patch_owner, patch_voxel, patch_live, voxel_mask, element_matrix):
    nz, ny = lax.axis_size("gz"), lax.axis_size("gy")
    devices = nz * ny

    send = pack(patch_owner, patch_live, patch_voxel, patch_force, devices)
    send, mask = lax.optimization_barrier((send, voxel_mask))
    recv = exchange(send)
    mask = jnp.concatenate([moved(mask[6:8], "gz", 1), mask, moved(mask[0:1], "gz", -1)], axis=0)
    mask = jnp.concatenate([moved(mask[:, 6:8], "gy", 1), mask, moved(mask[:, 0:1], "gy", -1)], axis=1)
    mask = mask.astype(F32)

    big = jnp.einsum("ij,lm->iljm", element_matrix, jnp.eye(LOADS, dtype=F32)).reshape(192, 192)
    rounded = lax.reduce_precision(big, 8, 7)
    k_high = rounded.astype(BF16)
    k_both = jnp.concatenate([k_high, (big - rounded).astype(BF16)], axis=0)
    flags = jnp.stack([lax.axis_index("gz") + 1 < nz, lax.axis_index("gy") + 1 < ny]).astype(F32)

    recv, mask, k_high, k_both, flags = lax.optimization_barrier((recv, mask, k_high, k_both, flags))
    field, z_low, z_high, y_low, y_high = scatter(recv)
    below, above = moved(z_high, "gz", 1), moved(z_low, "gz", -1)
    beside = (moved(y_high, "gy", 1), moved(y_low, "gy", -1))
    low = jnp.concatenate([below[:, 0:2], above[:, 0:2]], axis=0)
    high = jnp.concatenate([below[:, 6:8], above[:, 6:8]], axis=0)
    around = (field, below, above, *beside, moved(high, "gy", 1), moved(low, "gy", -1))
    s, q, gram = operator(flags, around, mask, k_both, k_high, devices)
    return final(exchange(gram), field, s, q)


def solution(mesh):
    placed = (
        P(AXES, None, None),
        P(AXES),
        P(AXES, None),
        P(AXES, None),
        P("gz", "gy", None),
        P(),
    )
    return jax.shard_map(
        body,
        mesh=mesh,
        in_specs=placed,
        out_specs=(P(None, "gz", "gy", None), P(None, "gz", "gy", None)),
        check_vma=False,
    )
```
